1024 devices in a mesh: rows: 16 (over z, core), cols: 64 (over x, y).
Axes of the slice: x: 8, y: 8, z: 8, core: 2. Of those that a mesh axis runs over, the one named last changes fastest.
Arguments:
- momentum_prev: float32 [8192, 8192], P('rows', 'cols'), may hold values from -170 to 170
- gradient: bfloat16 [8192, 8192], P('rows', 'cols'), may hold values from -6 to 6
- q_prev: float32 [8192, 512], P('cols'), may hold values from -0.0625 to 0.0625
Outputs:
- momentum_next: float32 [8192, 8192], P('rows', 'cols')
- q_next: float32 [8192, 512], P('cols')
- update: bfloat16 [8192, 8192], P('rows', 'cols')
The draws below stay inside these ranges and needn't reach their ends.
All inputs are finite; a program needn't handle non-finite values.
Results may differ from the reference program's by a relative error of at most 0.001.
Values sent between devices are 32-bit elements; how exact they have to be, the bound alone decides.
A program may use at most 32 MiB of HBM per device.

```python
import math
import jax
import jax.numpy as jnp
from jax import lax

D = 8192
RANK = 512


def draw_momentum_prev(key, part):
    key_base = jax.random.fold_in(key, 11)
    key_rows = jax.random.fold_in(key, 12)
    key_cols = jax.random.fold_in(key, 13)
    row_scale = jnp.exp(jax.random.uniform(key_rows, (D, 1), jnp.float32, 0.0, math.log(3.0)))
    col_scale = jnp.exp(jax.random.uniform(key_cols, (1, D), jnp.float32, 0.0, math.log(3.0)))
    rising = jnp.power(3.0, jnp.arange(D, dtype=jnp.float32) / D)[None, :]
    base = jnp.clip(jax.random.normal(key_base, (D, D), jnp.float32), -6.0, 6.0)
    return base * row_scale * col_scale * rising


def shard_levels(own_key, dims, split, low, high):
    factor_of, own = 1.0, jax.random.fold_in(own_key, 6)
    for position, parts in split:
        draws = jnp.exp(jax.random.uniform(jax.random.fold_in(own, position), (parts,), jnp.float32, low / len(split), high / len(split)))
        factor_of = factor_of * jnp.repeat(draws, dims[position] // parts).reshape([-1 if axis == position else 1 for axis in range(len(dims))])
    return factor_of


def scatter_about(key, dims, spread, reach, pieces=(), kind=jnp.bfloat16):
    array = spread * jax.random.normal(key, dims, jnp.float32)
    if pieces:
        array = array * shard_levels(key, dims, pieces, -0.22, 0.18)
    return jnp.clip(array, -reach, reach).astype(kind)


def setup_inputs(seed: int = 0) -> dict:
    splits = jax.random.split(jax.random.key(seed), 4)
    return {
        "momentum_prev": draw_momentum_prev(jax.random.fold_in(splits[3], 71), 0),
        "gradient": scatter_about(splits[1], (D, D), 1.0, 6.0, ((0, 16), (1, 64))),
        "q_prev": scatter_about(splits[2], (D, RANK), D ** -0.5, 0.0625, ((0, 64),), jnp.float32),
    }


def reference(momentum_prev, gradient, q_prev):
    highest = lax.Precision.HIGHEST
    momentum = 0.95 * momentum_prev + gradient.astype(jnp.float32)
    power = jnp.dot(momentum.astype(jnp.float32), q_prev.astype(jnp.float32), precision=highest, preferred_element_type=jnp.float32)
    gram = jnp.dot(power.T.astype(jnp.float32), power.astype(jnp.float32), precision=highest, preferred_element_type=jnp.float32)
    chol = jnp.linalg.cholesky(gram)
    basis = lax.linalg.triangular_solve(chol, power, left_side=False, lower=True, transpose_a=True)
    cross = jnp.dot(momentum.T.astype(jnp.float32), basis.astype(jnp.float32), precision=highest, preferred_element_type=jnp.float32)
    momentum_next = momentum - 0.5 * jnp.dot(basis.astype(jnp.float32), cross.T.astype(jnp.float32), precision=highest, preferred_element_type=jnp.float32)
    col_sq = lax.optimization_barrier(jnp.sum(cross * cross, axis=0))
    q_next = cross / (jnp.sqrt(col_sq) + 1e-08)
    factor = D / jnp.sqrt(jnp.float32(RANK))
    update = (factor * jnp.dot(basis.astype(jnp.float32), q_next.T.astype(jnp.float32), precision=highest, preferred_element_type=jnp.float32)).astype(jnp.bfloat16)
    return (momentum_next, q_next, update)
```

```python
import functools

import jax
import jax.numpy as jnp
from jax import lax
from jax.experimental import pallas as pl
from jax.experimental.pallas import tpu as pltpu
from jax.sharding import PartitionSpec as P

D = 8192
RANK = 512
HALF = RANK // 2
MESH = pl.DeviceIdType.MESH
VMEM = pltpu.VMEM
F32 = jnp.float32
HIGH = lax.Precision.HIGH


def order(n):
    return sorted(range(1, n), key=lambda d: -min(d, n - d))


class Grid:
    def __init__(self, nx, ny, nz):
        self.n = (nx, ny)
        self.nz = nz
        self.r = lax.axis_index("rows")
        self.c = lax.axis_index("cols")
        self.at = (lax.div(self.c, ny), lax.rem(self.c, ny))
        self.z, self.core = lax.div(self.r, 2), lax.rem(self.r, 2)

    def along(self, axis, d):
        return lax.rem(self.at[axis] + d, self.n[axis])

    def peer(self, axis, d):
        place = [self.at[0], self.at[1]]
        place[axis] = self.along(axis, d)
        return (self.r, place[0] * self.n[1] + place[1])

    def z_along(self, d):
        return lax.rem(self.z + d, self.nz)

    def z_peer(self, d):
        return (self.z_along(d) * 2 + self.core, self.c)

    def sibling(self):
        return (self.r + 1 - 2 * self.core, self.c)

    def plane_peers(self):
        return [self.peer(a, d) for a in (0, 1) for d in range(1, self.n[a])]

    def row_peers(self):
        return [self.sibling()] + [self.z_peer(d) for d in range(1, self.nz)]


def enter(peers):
    barrier = pltpu.get_barrier_semaphore()
    for device in peers:
        pl.semaphore_signal(barrier, inc=1, device_id=device, device_id_type=MESH)
    pl.semaphore_wait(barrier, len(peers))


def send(src, dst, sems, slot, device):
    copy = pltpu.make_async_remote_copy(
        src_ref=src,
        dst_ref=dst,
        send_sem=sems.at[(0,) + slot],
        recv_sem=sems.at[(1,) + slot],
        device_id=device,
        device_id_type=MESH,
    )
    copy.start()
    return copy


def power_kernel(nx, ny, nz, part, out, recv1, sum1, recv2, gather, sem1, sem2, sem3, sem4):
    g = Grid(nx, ny, nz)
    enter(g.plane_peers())
    rows = part.shape[0]
    big = [rows // g.n[h] for h in (0, 1)]
    small = [big[h] // g.n[1 - h] for h in (0, 1)]
    columns = [pl.ds(h * HALF, HALF) for h in (0, 1)]
    sent = []

    def block(i, size):
        return pl.ds(pl.multiple_of(i * size, size), size)

    first = [[], []]
    for h in (0, 1):
        for d in order(g.n[h]):
            first[h].append(
                send(
                    part.at[block(g.along(h, d), big[h]), columns[h]],
                    recv1.at[h, d - 1],
                    sem1,
                    (h, d - 1),
                    g.peer(h, d),
                )
            )
    second = [[], []]
    for h in (0, 1):
        total = part[block(g.at[h], big[h]), columns[h]]
        for copy in first[h]:
            copy.wait_recv()
        for d in range(1, g.n[h]):
            total = total + recv1[h, d - 1]
        sum1[h] = total
        for d in order(g.n[1 - h]):
            second[h].append(
                send(
                    sum1.at[h, block(g.along(1 - h, d), small[h])],
                    recv2.at[h, d - 1],
                    sem2,
                    (h, d - 1),
                    g.peer(1 - h, d),
                )
            )
    third = [[], []]
    for h in (0, 1):
        mine = block(g.at[1 - h], small[h])
        total = sum1[h, mine]
        for copy in second[h]:
            copy.wait_recv()
        for d in range(1, g.n[1 - h]):
            total = total + recv2[h, d - 1]
        gather[h, mine] = total
        for d in order(g.n[1 - h]):
            third[h].append(
                send(gather.at[h, mine], gather.at[h, mine], sem3, (h, d - 1), g.peer(1 - h, d))
            )
    fourth = [[], []]
    for h in (0, 1):
        for copy in third[h]:
            copy.wait_recv()
        mine = block(g.at[h], big[h])
        for d in order(g.n[h]):
            fourth[h].append(
                send(gather.at[h], out.at[mine, columns[h]], sem4, (h, d - 1), g.peer(h, d))
            )
        out[mine, columns[h]] = gather[h]
    for stage in (first, second, third, fourth):
        for h in (0, 1):
            for copy in stage[h]:
                copy.wait_send()
    for h in (0, 1):
        for copy in fourth[h]:
            copy.wait_recv()


def power_sum(nx, ny, nz, part):
    rows = part.shape[0]
    big, small = rows // nx, rows // nx // ny
    return pl.pallas_call(
        functools.partial(power_kernel, nx, ny, nz),
        name="power_sum",
        out_shape=jax.ShapeDtypeStruct((rows, RANK), F32),
        in_specs=[pl.BlockSpec(memory_space=VMEM)],
        out_specs=pl.BlockSpec(memory_space=VMEM),
        scratch_shapes=[
            VMEM((2, nx - 1, big, HALF), F32),
            VMEM((2, big, HALF), F32),
            VMEM((2, ny - 1, small, HALF), F32),
            VMEM((2, big, HALF), F32),
        ]
        + [pltpu.SemaphoreType.DMA((2, 2, nx - 1))] * 4,
        compiler_params=pltpu.CompilerParams(collective_id=0, has_side_effects=True),
    )(part)


def gram_kernel(
    nx, ny, nz, gram, cross, whole, crossed,
    gram_core, gram_z, cross_core, cross_sum, cross_z,
    core_sem, z_sem, plane_sem, back_sem,
):
    g = Grid(nx, ny, nz)
    enter(g.plane_peers() + g.row_peers())
    core, other = g.core, 1 - g.core
    x, y = g.at
    share = cross.shape[1] // nz

    def block(i):
        return pl.ds(pl.multiple_of(i * share, share), share)

    swap = [
        send(gram.at[other], gram_core, core_sem, (0,), g.sibling()),
        send(cross.at[other], cross_core, core_sem, (1,), g.sibling()),
    ]
    swap[0].wait_recv()
    gram_z[g.z] = gram[core] + gram_core[...]
    ups = []
    for d in order(nz):
        ups.append(send(gram_z.at[g.z], gram_z.at[g.z], z_sem, (0, d - 1), g.z_peer(d)))
    swap[1].wait_recv()
    cross_sum[...] = cross[core] + cross_core[...]
    shares = []
    for d in order(nz):
        shares.append(
            send(cross_sum.at[block(g.z_along(d))], cross_z.at[d - 1], z_sem, (1, d - 1), g.z_peer(d))
        )
    for copy in ups:
        copy.wait_recv()
    total = gram_z[0]
    for i in range(1, nz):
        total = total + gram_z[i]
    width = HALF // 2
    near = [[], []]
    for q in (0, 1):
        place = whole.at[core * 2 + q, x, y]
        whole[core * 2 + q, x, y] = total[:, q * width : (q + 1) * width]
        for d in order(g.n[1 - q]):
            near[q].append(send(place, place, plane_sem, (0, q, d - 1), g.peer(1 - q, d)))
    for copy in shares:
        copy.wait_recv()
    mine = block(g.z)
    total = cross_sum[mine]
    for d in range(1, nz):
        total = total + cross_z[d - 1]
    crossed[core, mine] = total
    gathers = []
    for d in order(nz):
        gathers.append(
            send(crossed.at[core, mine], crossed.at[core, mine], z_sem, (2, d - 1), g.z_peer(d))
        )
    far = [[], []]
    for q in (0, 1):
        for copy in near[q]:
            copy.wait_recv()
        place = whole.at[core * 2 + q, x] if q == 0 else whole.at[core * 2 + q, :, y]
        for d in order(g.n[q]):
            far[q].append(send(place, place, plane_sem, (1, q, d - 1), g.peer(q, d)))
    for copy in gathers:
        copy.wait_recv()
    back = [send(crossed.at[core], crossed.at[core], back_sem, (0,), g.sibling())]
    for q in (0, 1):
        for copy in far[q]:
            copy.wait_recv()
        place = whole.at[core * 2 + q]
        back.append(send(place, place, back_sem, (1 + q,), g.sibling()))
    for copy in swap + ups + shares + gathers + near[0] + near[1] + far[0] + far[1]:
        copy.wait_send()
    for copy in back:
        copy.wait()


def gram_sum(nx, ny, nz, gram, cross):
    rows, depth = gram.shape[1], cross.shape[1]
    return pl.pallas_call(
        functools.partial(gram_kernel, nx, ny, nz),
        name="gram_sum",
        out_shape=(
            jax.ShapeDtypeStruct((4, nx, ny, rows, HALF // 2), F32),
            jax.ShapeDtypeStruct((2, depth, HALF), F32),
        ),
        in_specs=[pl.BlockSpec(memory_space=VMEM)] * 2,
        out_specs=(pl.BlockSpec(memory_space=VMEM),) * 2,
        scratch_shapes=[
            VMEM((rows, HALF), F32),
            VMEM((nz, rows, HALF), F32),
            VMEM((depth, HALF), F32),
            VMEM((depth, HALF), F32),
            VMEM((nz - 1, depth // nz, HALF), F32),
            pltpu.SemaphoreType.DMA((2, 2)),
            pltpu.SemaphoreType.DMA((2, 3, nz - 1)),
            pltpu.SemaphoreType.DMA((2, 2, 2, nx - 1)),
            pltpu.SemaphoreType.DMA((2, 3)),
        ],
        compiler_params=pltpu.CompilerParams(collective_id=1, has_side_effects=True),
    )(gram, cross)


def norm_kernel(nx, ny, nz, part, out, recv, total, sems):
    g = Grid(nx, ny, nz)
    enter(g.plane_peers())
    copies = []
    total[...] = part[...]
    for axis in (0, 1):
        here = []
        for d in order(g.n[axis]):
            here.append(
                send(total.at[axis], recv.at[axis, d - 1], sems, (axis, d - 1), g.peer(axis, d))
            )
        for copy in here:
            copy.wait_recv()
        value = total[axis]
        for d in range(1, g.n[axis]):
            value = value + recv[axis, d - 1]
        if axis == 0:
            total[1] = value
        else:
            out[...] = value
        copies += here
    for copy in copies:
        copy.wait_send()


def norm_sum(nx, ny, nz, part):
    return pl.pallas_call(
        functools.partial(norm_kernel, nx, ny, nz),
        name="norm_sum",
        out_shape=jax.ShapeDtypeStruct((1, RANK), F32),
        in_specs=[pl.BlockSpec(memory_space=VMEM)],
        out_specs=pl.BlockSpec(memory_space=VMEM),
        scratch_shapes=[
            VMEM((2, nx - 1, 1, RANK), F32),
            VMEM((2, 1, RANK), F32),
            pltpu.SemaphoreType.DMA((2, 2, nx - 1)),
        ],
        compiler_params=pltpu.CompilerParams(collective_id=2, has_side_effects=True),
    )(jnp.broadcast_to(part, (2, 1, RANK)))


def dot(a, b, ca, cb):
    return lax.dot_general(
        a, b, (((ca,), (cb,)), ((), ())), precision=HIGH, preferred_element_type=F32
    )


def inverse_factor(gram):
    chol = jnp.linalg.cholesky(gram, symmetrize_input=False)
    return lax.linalg.triangular_solve(
        chol, jnp.eye(RANK, dtype=F32), left_side=True, lower=True
    )


def body(nx, ny, nz, momentum_prev, gradient, q_prev):
    momentum = 0.95 * momentum_prev + gradient.astype(F32)
    power = power_sum(nx, ny, nz, dot(momentum, q_prev, 1, 0))
    rows = RANK // (nx * ny)
    mine = lax.dynamic_slice(power, (0, rows * lax.axis_index("cols")), (power.shape[0], rows))
    gram_part = dot(mine, power, 0, 0).reshape(rows, 2, HALF).transpose(1, 0, 2)
    depth = momentum.shape[1]
    cross_part = dot(momentum, power, 0, 0).reshape(depth, 2, HALF).transpose(1, 0, 2)
    gram, crossed = gram_sum(nx, ny, nz, gram_part, cross_part)
    gram = gram.reshape(4, RANK, RANK // 4).transpose(1, 0, 2).reshape(RANK, RANK)
    crossed = crossed.transpose(1, 0, 2).reshape(depth, RANK)
    inverse = inverse_factor(gram)
    cross = dot(crossed, inverse, 1, 1)
    col_sq = norm_sum(nx, ny, nz, jnp.sum(cross * cross, axis=0, keepdims=True))
    q_next = cross / (jnp.sqrt(col_sq) + 1e-08)
    factor = D / jnp.sqrt(jnp.float32(RANK))
    both = jnp.concatenate([-0.5 * cross, factor * q_next], axis=0)
    product = dot(power, dot(inverse, both, 0, 1), 1, 0)
    return (
        momentum + product[:, :depth],
        q_next,
        product[:, depth:].astype(jnp.bfloat16),
    )


def sizes(mesh):
    side = {64: 8, 16: 4, 4: 2}[mesh.shape["cols"]]
    return side, side, mesh.shape["rows"] // 2


def solution(mesh):
    in_specs = (P("rows", "cols"), P("rows", "cols"), P("cols", None))
    out_specs = (P("rows", "cols"), P("cols", None), P("rows", "cols"))
    return jax.shard_map(
        functools.partial(body, *sizes(mesh)),
        mesh=mesh,
        in_specs=in_specs,
        out_specs=out_specs,
        check_vma=False,
    )
```

```python
import functools

import jax
import jax.numpy as jnp
from jax import lax
from jax.experimental import pallas as pl
from jax.experimental.pallas import tpu as pltpu
from jax.sharding import PartitionSpec as P

D = 8192
RANK = 512
HALF = RANK // 2
BLOCK = 128
MESH = pl.DeviceIdType.MESH
VMEM = pltpu.VMEM
F32 = jnp.float32
HIGH = lax.Precision.HIGH


def order(n):
    return sorted(range(1, n), key=lambda d: -min(d, n - d))


class Grid:
    def __init__(self, nx, ny, nz):
        self.n = (nx, ny)
        self.nz = nz
        self.r = lax.axis_index("rows")
        self.c = lax.axis_index("cols")
        self.at = (lax.div(self.c, ny), lax.rem(self.c, ny))
        self.z, self.core = lax.div(self.r, 2), lax.rem(self.r, 2)

    def along(self, axis, d):
        return lax.rem(self.at[axis] + d, self.n[axis])

    def peer(self, axis, d):
        place = [self.at[0], self.at[1]]
        place[axis] = self.along(axis, d)
        return (self.r, place[0] * self.n[1] + place[1])

    def z_along(self, d):
        return lax.rem(self.z + d, self.nz)

    def z_peer(self, d):
        return (self.z_along(d) * 2 + self.core, self.c)

    def sibling(self):
        return (self.r + 1 - 2 * self.core, self.c)

    def plane_peers(self):
        return [self.peer(a, d) for a in (0, 1) for d in range(1, self.n[a])]

    def row_peers(self):
        return [self.sibling()] + [self.z_peer(d) for d in range(1, self.nz)]


def enter(peers):
    barrier = pltpu.get_barrier_semaphore()
    for device in peers:
        pl.semaphore_signal(barrier, inc=1, device_id=device, device_id_type=MESH)
    pl.semaphore_wait(barrier, len(peers))


def send(src, dst, sems, slot, device):
    copy = pltpu.make_async_remote_copy(
        src_ref=src,
        dst_ref=dst,
        send_sem=sems.at[(0,) + slot],
        recv_sem=sems.at[(1,) + slot],
        device_id=device,
        device_id_type=MESH,
    )
    copy.start()
    return copy


def split(a):
    high = a.astype(jnp.bfloat16)
    return high, (a - high.astype(F32)).astype(jnp.bfloat16)


def dot3(a, b, ca, cb):
    (a_high, a_low), (b_high, b_low) = split(a), split(b)

    def one(p, q):
        return lax.dot_general(p, q, (((ca,), (cb,)), ((), ())), preferred_element_type=F32)

    return one(a_high, b_high) + (one(a_high, b_low) + one(a_low, b_high))


def power_kernel(nx, ny, nz, part, out, recv1, sum1, recv2, gather, sem1, sem2, sem3, sem4):
    g = Grid(nx, ny, nz)
    enter(g.plane_peers())
    rows = part.shape[0]
    big = [rows // g.n[h] for h in (0, 1)]
    small = [big[h] // g.n[1 - h] for h in (0, 1)]
    columns = [pl.ds(h * HALF, HALF) for h in (0, 1)]
    sent = []

    def block(i, size):
        return pl.ds(pl.multiple_of(i * size, size), size)

    first = [[], []]
    for h in (0, 1):
        for d in order(g.n[h]):
            first[h].append(
                send(
                    part.at[block(g.along(h, d), big[h]), columns[h]],
                    recv1.at[h, d - 1],
                    sem1,
                    (h, d - 1),
                    g.peer(h, d),
                )
            )
    second = [[], []]
    for h in (0, 1):
        total = part[block(g.at[h], big[h]), columns[h]]
        for copy in first[h]:
            copy.wait_recv()
        for d in range(1, g.n[h]):
            total = total + recv1[h, d - 1]
        sum1[h] = total
        for d in order(g.n[1 - h]):
            second[h].append(
                send(
                    sum1.at[h, block(g.along(1 - h, d), small[h])],
                    recv2.at[h, d - 1],
                    sem2,
                    (h, d - 1),
                    g.peer(1 - h, d),
                )
            )
    third = [[], []]
    for h in (0, 1):
        mine = block(g.at[1 - h], small[h])
        total = sum1[h, mine]
        for copy in second[h]:
            copy.wait_recv()
        for d in range(1, g.n[1 - h]):
            total = total + recv2[h, d - 1]
        gather[h, mine] = total
        for d in order(g.n[1 - h]):
            third[h].append(
                send(gather.at[h, mine], gather.at[h, mine], sem3, (h, d - 1), g.peer(1 - h, d))
            )
    fourth = [[], []]
    for h in (0, 1):
        for copy in third[h]:
            copy.wait_recv()
        mine = block(g.at[h], big[h])
        for d in order(g.n[h]):
            fourth[h].append(
                send(gather.at[h], out.at[mine, columns[h]], sem4, (h, d - 1), g.peer(h, d))
            )
        out[mine, columns[h]] = gather[h]
    for stage in (first, second, third, fourth):
        for h in (0, 1):
            for copy in stage[h]:
                copy.wait_send()
    for h in (0, 1):
        for copy in fourth[h]:
            copy.wait_recv()


def power_sum(nx, ny, nz, part):
    rows = part.shape[0]
    big, small = rows // nx, rows // nx // ny
    return pl.pallas_call(
        functools.partial(power_kernel, nx, ny, nz),
        name="power_sum",
        out_shape=jax.ShapeDtypeStruct((rows, RANK), F32),
        in_specs=[pl.BlockSpec(memory_space=VMEM)],
        out_specs=pl.BlockSpec(memory_space=VMEM),
        scratch_shapes=[
            VMEM((2, nx - 1, big, HALF), F32),
            VMEM((2, big, HALF), F32),
            VMEM((2, ny - 1, small, HALF), F32),
            VMEM((2, big, HALF), F32),
        ]
        + [pltpu.SemaphoreType.DMA((2, 2, nx - 1))] * 4,
        compiler_params=pltpu.CompilerParams(collective_id=0, has_side_effects=True),
    )(part)


def gram_kernel(
    nx, ny, nz, gram, momentum, power, whole, crossed,
    gram_core, gram_z, cross, cross_core, cross_sum, cross_z,
    core_sem, z_sem, plane_sem, back_sem,
):
    g = Grid(nx, ny, nz)
    enter(g.plane_peers() + g.row_peers())
    core = g.core
    x, y = g.at
    share = cross.shape[0] // nz
    own = pl.ds(pl.multiple_of(core * HALF, HALF), HALF)
    other = pl.ds(pl.multiple_of((1 - core) * HALF, HALF), HALF)

    def block(i):
        return pl.ds(pl.multiple_of(i * share, share), share)

    swap = [send(gram.at[:, other], gram_core, core_sem, (0,), g.sibling())]
    cross[...] = dot3(momentum[...], power[...], 0, 0)
    swap.append(send(cross.at[:, other], cross_core, core_sem, (1,), g.sibling()))
    swap[0].wait_recv()
    gram_z[g.z] = gram[:, own] + gram_core[...]
    ups = []
    for d in order(nz):
        ups.append(send(gram_z.at[g.z], gram_z.at[g.z], z_sem, (0, d - 1), g.z_peer(d)))
    swap[1].wait_recv()
    cross_sum[...] = cross[:, own] + cross_core[...]
    shares = []
    for d in order(nz):
        shares.append(
            send(cross_sum.at[block(g.z_along(d))], cross_z.at[d - 1], z_sem, (1, d - 1), g.z_peer(d))
        )
    for copy in ups:
        copy.wait_recv()
    total = gram_z[0]
    for i in range(1, nz):
        total = total + gram_z[i]
    width = HALF // 2
    near = [[], []]
    for q in (0, 1):
        place = whole.at[core * 2 + q, x, y]
        whole[core * 2 + q, x, y] = total[:, q * width : (q + 1) * width]
        for d in order(g.n[1 - q]):
            near[q].append(send(place, place, plane_sem, (0, q, d - 1), g.peer(1 - q, d)))
    for copy in shares:
        copy.wait_recv()
    mine = block(g.z)
    total = cross_sum[mine]
    for d in range(1, nz):
        total = total + cross_z[d - 1]
    crossed[mine, own] = total
    gathers = []
    for d in order(nz):
        gathers.append(
            send(crossed.at[mine, own], crossed.at[mine, own], z_sem, (2, d - 1), g.z_peer(d))
        )
    far = [[], []]
    for q in (0, 1):
        for copy in near[q]:
            copy.wait_recv()
        place = whole.at[core * 2 + q, x] if q == 0 else whole.at[core * 2 + q, :, y]
        for d in order(g.n[q]):
            far[q].append(send(place, place, plane_sem, (1, q, d - 1), g.peer(q, d)))
    for copy in gathers:
        copy.wait_recv()
    back = [send(crossed.at[:, own], crossed.at[:, own], back_sem, (0,), g.sibling())]
    for q in (0, 1):
        for copy in far[q]:
            copy.wait_recv()
        place = whole.at[core * 2 + q]
        back.append(send(place, place, back_sem, (1 + q,), g.sibling()))
    for copy in swap + ups + shares + gathers + near[0] + near[1] + far[0] + far[1]:
        copy.wait_send()
    for copy in back:
        copy.wait()


def gram_sum(nx, ny, nz, gram, momentum, power):
    rows, depth = gram.shape[0], momentum.shape[1]
    return pl.pallas_call(
        functools.partial(gram_kernel, nx, ny, nz),
        name="gram_sum",
        out_shape=(
            jax.ShapeDtypeStruct((4, nx, ny, rows, HALF // 2), F32),
            jax.ShapeDtypeStruct((depth, RANK), F32),
        ),
        in_specs=[pl.BlockSpec(memory_space=VMEM)] * 3,
        out_specs=(pl.BlockSpec(memory_space=VMEM),) * 2,
        scratch_shapes=[
            VMEM((rows, HALF), F32),
            VMEM((nz, rows, HALF), F32),
            VMEM((depth, RANK), F32),
            VMEM((depth, HALF), F32),
            VMEM((depth, HALF), F32),
            VMEM((nz - 1, depth // nz, HALF), F32),
            pltpu.SemaphoreType.DMA((2, 2)),
            pltpu.SemaphoreType.DMA((2, 3, nz - 1)),
            pltpu.SemaphoreType.DMA((2, 2, 2, nx - 1)),
            pltpu.SemaphoreType.DMA((2, 3)),
        ],
        compiler_params=pltpu.CompilerParams(collective_id=1, has_side_effects=True),
    )(gram, momentum, power)


def norm_kernel(nx, ny, nz, part, out, recv, total, sems):
    g = Grid(nx, ny, nz)
    enter(g.plane_peers())
    copies = []
    total[...] = part[...]
    for axis in (0, 1):
        here = []
        for d in order(g.n[axis]):
            here.append(
                send(total.at[axis], recv.at[axis, d - 1], sems, (axis, d - 1), g.peer(axis, d))
            )
        for copy in here:
            copy.wait_recv()
        value = total[axis]
        for d in range(1, g.n[axis]):
            value = value + recv[axis, d - 1]
        if axis == 0:
            total[1] = value
        else:
            out[...] = value
        copies += here
    for copy in copies:
        copy.wait_send()


def norm_sum(nx, ny, nz, part):
    return pl.pallas_call(
        functools.partial(norm_kernel, nx, ny, nz),
        name="norm_sum",
        out_shape=jax.ShapeDtypeStruct((1, RANK), F32),
        in_specs=[pl.BlockSpec(memory_space=VMEM)],
        out_specs=pl.BlockSpec(memory_space=VMEM),
        scratch_shapes=[
            VMEM((2, nx - 1, 1, RANK), F32),
            VMEM((2, 1, RANK), F32),
            pltpu.SemaphoreType.DMA((2, 2, nx - 1)),
        ],
        compiler_params=pltpu.CompilerParams(collective_id=2, has_side_effects=True),
    )(part)


def dot(a, b, ca, cb):
    return lax.dot_general(
        a, b, (((ca,), (cb,)), ((), ())), precision=HIGH, preferred_element_type=F32
    )


def rowcast(x, k):
    return jnp.broadcast_to(x[k : k + 1, :], (8, BLOCK))


def factor_block(a, x):
    lane = lax.broadcasted_iota(jnp.int32, (8, BLOCK), 1)
    sub = lax.broadcasted_iota(jnp.int32, (8, BLOCK), 0)
    tiles = BLOCK // 8
    for t in range(tiles):
        x[8 * t : 8 * t + 8, :] = jnp.where(lane == sub + 8 * t, 1.0, 0.0)
    for t in range(tiles):
        rows = a[8 * t : 8 * t + 8, :]
        inverse = x[8 * t : 8 * t + 8, :]
        columns = [jnp.broadcast_to(rows[:, 8 * t + k : 8 * t + k + 1], (8, BLOCK)) for k in range(8)]
        done = inverse
        pivots, ahead, row_a, row_x = [], [], [], []
        for k in range(8):
            root = lax.rsqrt(rowcast(columns[k], k))
            pivots.append(root)
            row_a.append(rowcast(rows, k) * root)
            row_x.append(rowcast(inverse, k) * root)
            done = jnp.where(sub == k, row_x[k], done)
            ahead.append([rowcast(columns[l], k) * root for l in range(k + 1, 8)])
            if k == 7:
                break
            weight = jnp.where(sub > k, columns[k] * root, 0.0)
            for l in range(k + 1, 8):
                columns[l] = columns[l] - weight * ahead[k][l - k - 1]
            rows = rows - weight * row_a[k]
            inverse = inverse - weight * row_x[k]
        x[8 * t : 8 * t + 8, :] = done
        for s in range(t + 1, tiles):
            rest = a[8 * s : 8 * s + 8, :]
            rest_x = x[8 * s : 8 * s + 8, :]
            columns = [
                jnp.broadcast_to(rest[:, 8 * t + k : 8 * t + k + 1], (8, BLOCK)) for k in range(8)
            ]
            for k in range(8):
                weight = columns[k] * pivots[k]
                rest = rest - weight * row_a[k]
                rest_x = rest_x - weight * row_x[k]
                for l in range(k + 1, 8):
                    columns[l] = columns[l] - weight * ahead[k][l - k - 1]
            a[8 * s : 8 * s + 8, :] = rest
            x[8 * s : 8 * s + 8, :] = rest_x


def full_dot(a, b, ca, cb):
    return lax.dot_general(
        a, b, (((ca,), (cb,)), ((), ())), precision=lax.Precision.HIGHEST, preferred_element_type=F32
    )


def inverse_kernel(gram, crossed, out, cross, col_sq, a, block, small):
    a[...] = gram[...]
    out[...] = jnp.zeros_like(out)

    @pl.loop(0, RANK // BLOCK)
    def _(step):
        block[...] = a[step, pl.ds(pl.multiple_of(step * BLOCK, BLOCK), BLOCK), :]
        factor_block(block, small)
        for i in range(RANK // BLOCK):

            @pl.when(step == i)
            def _():
                low, high = i * BLOCK, (i + 1) * BLOCK
                diagonal = small[...]
                out[low:high, low:high] = diagonal
                if i:
                    out[low:high, :low] = full_dot(diagonal, out[low:high, :low], 1, 0)
                if high < RANK:
                    below = full_dot(a[i, high:, :], diagonal, 1, 1)
                    for j in range(i + 1, RANK // BLOCK):
                        top = (j - i - 1) * BLOCK
                        a[j, j * BLOCK :, :] -= full_dot(
                            below[top:], below[top : top + BLOCK], 1, 1
                        )
                    out[high:, :high] -= full_dot(below, out[low:high, :high], 1, 0)

    value = dot3(crossed[...], out[...], 1, 1)
    cross[...] = value
    col_sq[...] = jnp.broadcast_to(jnp.sum(value * value, axis=0, keepdims=True), (2, 1, RANK))


def inverse_factor(gram, crossed):
    depth = crossed.shape[0]
    return pl.pallas_call(
        inverse_kernel,
        name="inverse_factor",
        out_shape=(
            jax.ShapeDtypeStruct((RANK, RANK), F32),
            jax.ShapeDtypeStruct((depth, RANK), F32),
            jax.ShapeDtypeStruct((2, 1, RANK), F32),
        ),
        in_specs=[pl.BlockSpec(memory_space=VMEM)] * 2,
        out_specs=(pl.BlockSpec(memory_space=VMEM),) * 3,
        scratch_shapes=[
            VMEM((RANK // BLOCK, RANK, BLOCK), F32),
            VMEM((BLOCK, BLOCK), F32),
            VMEM((BLOCK, BLOCK), F32),
        ],
    )(gram, crossed)


def body(nx, ny, nz, momentum_prev, gradient, q_prev):
    momentum = 0.95 * momentum_prev + gradient.astype(F32)
    power = power_sum(nx, ny, nz, dot(momentum, q_prev, 1, 0))
    rows = RANK // (nx * ny)
    mine = lax.dynamic_slice(power, (0, rows * lax.axis_index("cols")), (power.shape[0], rows))
    gram, crossed = gram_sum(nx, ny, nz, dot(mine, power, 0, 0), momentum, power)
    inverse, cross, col_sq = inverse_factor(gram.reshape(4, RANK, RANK // 4), crossed)
    col_sq = norm_sum(nx, ny, nz, col_sq)
    q_next = cross / (jnp.sqrt(col_sq) + 1e-08)
    factor = D / jnp.sqrt(jnp.float32(RANK))
    both = jnp.concatenate([-0.5 * cross, factor * q_next], axis=0)
    depth = cross.shape[0]
    product = dot(power, dot(inverse, both, 0, 1), 1, 0)
    return (
        momentum + product[:, :depth],
        q_next,
        product[:, depth:].astype(jnp.bfloat16),
    )


def sizes(mesh):
    side = {64: 8, 16: 4, 4: 2}[mesh.shape["cols"]]
    return side, side, mesh.shape["rows"] // 2


def solution(mesh):
    in_specs = (P("rows", "cols"), P("rows", "cols"), P("cols", None))
    out_specs = (P("rows", "cols"), P("cols", None), P("rows", "cols"))
    return jax.shard_map(
        functools.partial(body, *sizes(mesh)),
        mesh=mesh,
        in_specs=in_specs,
        out_specs=out_specs,
        check_vma=False,
    )
```

```python
import functools

import jax
import jax.numpy as jnp
from jax import lax
from jax.experimental import pallas as pl
from jax.experimental.pallas import tpu as pltpu
from jax.sharding import PartitionSpec as P

D = 8192
RANK = 512
HALF = RANK // 2
BLOCK = 128
MESH = pl.DeviceIdType.MESH
VMEM = pltpu.VMEM
F32 = jnp.float32
FACTOR = D / RANK**0.5


def order(n):
    return sorted(range(1, n), key=lambda d: -min(d, n - d))


class Grid:
    def __init__(self, nx, ny, nz):
        self.n = (nx, ny)
        self.nz = nz
        self.r = lax.axis_index("rows")
        self.c = lax.axis_index("cols")
        self.at = (lax.div(self.c, ny), lax.rem(self.c, ny))
        self.z, self.core = lax.div(self.r, 2), lax.rem(self.r, 2)

    def along(self, axis, d):
        return lax.rem(self.at[axis] + d, self.n[axis])

    def peer(self, axis, d):
        place = [self.at[0], self.at[1]]
        place[axis] = self.along(axis, d)
        return (self.r, place[0] * self.n[1] + place[1])

    def z_along(self, d):
        return lax.rem(self.z + d, self.nz)

    def z_peer(self, d):
        return (self.z_along(d) * 2 + self.core, self.c)

    def sibling(self):
        return (self.r + 1 - 2 * self.core, self.c)

    def plane_peers(self):
        return [self.peer(a, d) for a in (0, 1) for d in range(1, self.n[a])]

    def row_peers(self):
        return [self.sibling()] + [self.z_peer(d) for d in range(1, self.nz)]


def greet(peers):
    barrier = pltpu.get_barrier_semaphore()
    for device in peers:
        pl.semaphore_signal(barrier, inc=1, device_id=device, device_id_type=MESH)
    return lambda: pl.semaphore_wait(barrier, len(peers))


def send(src, dst, sems, slot, device):
    copy = pltpu.make_async_remote_copy(
        src_ref=src,
        dst_ref=dst,
        send_sem=sems.at[(0,) + slot],
        recv_sem=sems.at[(1,) + slot],
        device_id=device,
        device_id_type=MESH,
    )
    copy.start()
    return copy


def rowcast(x, k):
    return jnp.broadcast_to(x[k : k + 1, :], (8, BLOCK))


def factor_block(a, x):
    lane = lax.broadcasted_iota(jnp.int32, (8, BLOCK), 1)
    sub = lax.broadcasted_iota(jnp.int32, (8, BLOCK), 0)
    tiles = BLOCK // 8
    for t in range(tiles):
        x[8 * t : 8 * t + 8, :] = jnp.where(lane == sub + 8 * t, 1.0, 0.0)
    for t in range(tiles):
        rows = a[8 * t : 8 * t + 8, :]
        inverse = x[8 * t : 8 * t + 8, :]
        columns = [jnp.broadcast_to(rows[:, 8 * t + k : 8 * t + k + 1], (8, BLOCK)) for k in range(8)]
        done = inverse
        pivots, ahead, row_a, row_x = [], [], [], []
        for k in range(8):
            root = lax.rsqrt(rowcast(columns[k], k))
            pivots.append(root)
            row_a.append(rowcast(rows, k) * root)
            row_x.append(rowcast(inverse, k) * root)
            done = jnp.where(sub == k, row_x[k], done)
            ahead.append([rowcast(columns[l], k) * root for l in range(k + 1, 8)])
            if k == 7:
                break
            weight = jnp.where(sub > k, columns[k] * root, 0.0)
            for l in range(k + 1, 8):
                columns[l] = columns[l] - weight * ahead[k][l - k - 1]
            rows = rows - weight * row_a[k]
            inverse = inverse - weight * row_x[k]
        x[8 * t : 8 * t + 8, :] = done
        for s in range(t + 1, tiles):
            rest = a[8 * s : 8 * s + 8, :]
            rest_x = x[8 * s : 8 * s + 8, :]
            columns = [
                jnp.broadcast_to(rest[:, 8 * t + k : 8 * t + k + 1], (8, BLOCK)) for k in range(8)
            ]
            for k in range(8):
                weight = columns[k] * pivots[k]
                rest = rest - weight * row_a[k]
                rest_x = rest_x - weight * row_x[k]
                for l in range(k + 1, 8):
                    columns[l] = columns[l] - weight * ahead[k][l - k - 1]
            a[8 * s : 8 * s + 8, :] = rest
            x[8 * s : 8 * s + 8, :] = rest_x


def full_dot(a, b, ca, cb):
    return lax.dot_general(
        a, b, (((ca,), (cb,)), ((), ())), precision=lax.Precision.HIGHEST, preferred_element_type=F32
    )


def block(i, size):
    return pl.ds(pl.multiple_of(i * size, size), size)


def arrived(copies):
    for copy in copies:
        copy.wait_recv()


def sum_power(g, part, power, recv1, sum1, recv2, gather, sems):
    rows = part.shape[0]
    big = [rows // g.n[h] for h in (0, 1)]
    small = [big[h] // g.n[1 - h] for h in (0, 1)]
    columns = [pl.ds(h * HALF, HALF) for h in (0, 1)]
    first, second, third, fourth = [[], []], [[], []], [[], []], [[], []]
    for h in (0, 1):
        for d in order(g.n[h]):
            source = part.at[block(g.along(h, d), big[h]), columns[h]]
            first[h].append(send(source, recv1.at[h, d - 1], sems, (0, h, d - 1), g.peer(h, d)))
    for h in (0, 1):
        total = part[block(g.at[h], big[h]), columns[h]]
        arrived(first[h])
        for d in range(1, g.n[h]):
            total = total + recv1[h, d - 1]
        sum1[h] = total
        for d in order(g.n[1 - h]):
            source = sum1.at[h, block(g.along(1 - h, d), small[h])]
            second[h].append(
                send(source, recv2.at[h, d - 1], sems, (1, h, d - 1), g.peer(1 - h, d))
            )
    for h in (0, 1):
        mine = block(g.at[1 - h], small[h])
        total = sum1[h, mine]
        arrived(second[h])
        for d in range(1, g.n[1 - h]):
            total = total + recv2[h, d - 1]
        gather[h, mine] = total
        place = gather.at[h, mine]
        for d in order(g.n[1 - h]):
            third[h].append(send(place, place, sems, (2, h, d - 1), g.peer(1 - h, d)))
    for h in (0, 1):
        arrived(third[h])
        mine = block(g.at[h], big[h])
        for d in order(g.n[h]):
            place = power.at[mine, columns[h]]
            fourth[h].append(send(gather.at[h], place, sems, (3, h, d - 1), g.peer(h, d)))
        power[mine, columns[h]] = gather[h]
    for h in (0, 1):
        arrived(fourth[h])
    return sum(first + second + third + fourth, [])


def factor_gram(a, out, tile, small):
    out[...] = jnp.zeros_like(out)

    @pl.loop(0, RANK // BLOCK)
    def _(step):
        tile[...] = a[step, block(step, BLOCK), :]
        factor_block(tile, small)
        for i in range(RANK // BLOCK):

            @pl.when(step == i)
            def _():
                low, high = i * BLOCK, (i + 1) * BLOCK
                diagonal = small[...]
                out[low:high, low:high] = diagonal
                if i:
                    out[low:high, :low] = full_dot(diagonal, out[low:high, :low], 1, 0)
                if high < RANK:
                    below = full_dot(a[i, high:, :], diagonal, 1, 1)
                    for j in range(i + 1, RANK // BLOCK):
                        top = (j - i - 1) * BLOCK
                        a[j, j * BLOCK :, :] -= full_dot(
                            below[top:], below[top : top + BLOCK], 1, 1
                        )
                    out[high:, :high] -= full_dot(below, out[low:high, :high], 1, 0)


def step_kernel(
    nx, ny, nz, previous, gradient, q_prev, momentum_next, q_next, update,
    momentum, part, power, recv1, sum1, recv2, gather,
    slab, gram_core, gram_z, whole, a, tile, small, inverse,
    local, cross_core, cross_sum, cross_z, crossed, cross, squares, squares_recv,
    power_sem, core_sem, z_sem, plane_sem, back_sem, norm_sem,
):
    g = Grid(nx, ny, nz)
    x, y = g.at
    core = g.core
    ready = greet(g.plane_peers() + g.row_peers())
    momentum[...] = 0.95 * previous[...] + gradient[...].astype(F32)
    part[...] = full_dot(momentum[...], q_prev[...], 1, 0)
    ready()
    sent = sum_power(g, part, power, recv1, sum1, recv2, gather, power_sem)

    rows = RANK // (nx * ny)
    share = local.shape[0] // nz
    own, other = block(core, HALF), block(1 - core, HALF)
    first = g.c * rows
    slab[...] = full_dot(power[:, block(lax.div(first, BLOCK), BLOCK)], power[...], 0, 0)
    mine = pl.ds(pl.multiple_of(lax.rem(first, BLOCK), rows), rows)
    swap = [send(slab.at[mine, other], gram_core, core_sem, (0,), g.sibling())]
    local[...] = full_dot(momentum[...], power[...], 0, 0)
    swap.append(send(local.at[:, other], cross_core, core_sem, (1,), g.sibling()))
    swap[0].wait_recv()
    gram_z[g.z] = slab[mine, own] + gram_core[...]
    ups = []
    for d in order(nz):
        ups.append(send(gram_z.at[g.z], gram_z.at[g.z], z_sem, (0, d - 1), g.z_peer(d)))
    swap[1].wait_recv()
    cross_sum[...] = local[:, own] + cross_core[...]
    shares = []
    for d in order(nz):
        source = cross_sum.at[block(g.z_along(d), share)]
        shares.append(send(source, cross_z.at[d - 1], z_sem, (1, d - 1), g.z_peer(d)))
    arrived(ups)
    total = gram_z[0]
    for i in range(1, nz):
        total = total + gram_z[i]
    near, far = [[], []], [[], []]
    for q in (0, 1):
        place = whole.at[core * 2 + q, x, y]
        whole[core * 2 + q, x, y] = total[:, q * BLOCK : (q + 1) * BLOCK]
        for d in order(g.n[1 - q]):
            near[q].append(send(place, place, plane_sem, (0, q, d - 1), g.peer(1 - q, d)))
    arrived(shares)
    mine = block(g.z, share)
    total = cross_sum[mine]
    for d in range(1, nz):
        total = total + cross_z[d - 1]
    crossed[mine, own] = total
    gathers = []
    place = crossed.at[mine, own]
    for d in order(nz):
        gathers.append(send(place, place, z_sem, (2, d - 1), g.z_peer(d)))
    for q in (0, 1):
        arrived(near[q])
        place = whole.at[core * 2 + q, x] if q == 0 else whole.at[core * 2 + q, :, y]
        for d in order(g.n[q]):
            far[q].append(send(place, place, plane_sem, (1, q, d - 1), g.peer(q, d)))
    arrived(gathers)
    place = crossed.at[:, own]
    back = [send(place, place, back_sem, (0,), g.sibling())]
    for q in (0, 1):
        arrived(far[q])
        place = whole.at[core * 2 + q]
        back.append(send(place, place, back_sem, (1 + q,), g.sibling()))
    arrived(back[1:])

    a[...] = whole[...].reshape(a.shape)
    factor_gram(a, inverse, tile, small)
    arrived(back[:1])

    cross[...] = full_dot(crossed[...], inverse[...], 1, 1)
    squares[0] = jnp.sum(cross[...] * cross[...], axis=0, keepdims=True)
    norms = [[], []]
    for axis in (0, 1):
        for d in order(g.n[axis]):
            place = squares_recv.at[axis, d - 1]
            norms[axis].append(
                send(squares.at[axis], place, norm_sem, (axis, d - 1), g.peer(axis, d))
            )
        if axis == 0:
            turned = full_dot(inverse[...], -0.5 * cross[...], 0, 1)
            momentum_next[...] = momentum[...] + full_dot(power[...], turned, 1, 0)
        arrived(norms[axis])
        total = squares[axis]
        for d in range(1, g.n[axis]):
            total = total + squares_recv[axis, d - 1]
        if axis == 0:
            squares[1] = total
    value = cross[...] / (jnp.sqrt(total) + 1e-08)
    q_next[...] = value
    turned = full_dot(inverse[...], FACTOR * value, 0, 1)
    update[...] = full_dot(power[...], turned, 1, 0).astype(update.dtype)
    for copy in sent + swap + ups + shares + gathers + near[0] + near[1] + far[0] + far[1] + back:
        copy.wait_send()
    for copy in norms[0] + norms[1]:
        copy.wait_send()


def body(nx, ny, nz, previous, gradient, q_prev):
    height, depth = previous.shape
    rows = RANK // (nx * ny)
    big, small = height // nx, height // (nx * ny)
    dma = pltpu.SemaphoreType.DMA
    return pl.pallas_call(
        functools.partial(step_kernel, nx, ny, nz),
        name="power_step",
        out_shape=(
            jax.ShapeDtypeStruct((height, depth), F32),
            jax.ShapeDtypeStruct((depth, RANK), F32),
            jax.ShapeDtypeStruct((height, depth), jnp.bfloat16),
        ),
        in_specs=[pl.BlockSpec(memory_space=VMEM)] * 3,
        out_specs=(pl.BlockSpec(memory_space=VMEM),) * 3,
        scratch_shapes=[
            VMEM((height, depth), F32),
            VMEM((height, RANK), F32),
            VMEM((height, RANK), F32),
            VMEM((2, nx - 1, big, HALF), F32),
            VMEM((2, big, HALF), F32),
            VMEM((2, ny - 1, small, HALF), F32),
            VMEM((2, big, HALF), F32),
            VMEM((BLOCK, RANK), F32),
            VMEM((rows, HALF), F32),
            VMEM((nz, rows, HALF), F32),
            VMEM((RANK // BLOCK, nx, ny, rows, BLOCK), F32),
            VMEM((RANK // BLOCK, RANK, BLOCK), F32),
            VMEM((BLOCK, BLOCK), F32),
            VMEM((BLOCK, BLOCK), F32),
            VMEM((RANK, RANK), F32),
            VMEM((depth, RANK), F32),
            VMEM((depth, HALF), F32),
            VMEM((depth, HALF), F32),
            VMEM((nz - 1, depth // nz, HALF), F32),
            VMEM((depth, RANK), F32),
            VMEM((depth, RANK), F32),
            VMEM((2, 1, RANK), F32),
            VMEM((2, nx - 1, 1, RANK), F32),
            dma((2, 4, 2, nx - 1)),
            dma((2, 2)),
            dma((2, 3, nz - 1)),
            dma((2, 2, 2, nx - 1)),
            dma((2, 3)),
            dma((2, 2, nx - 1)),
        ],
        compiler_params=pltpu.CompilerParams(
            collective_id=0, has_side_effects=True, vmem_limit_bytes=60 << 20
        ),
    )(previous, gradient, q_prev)


def sizes(mesh):
    side = {64: 8, 16: 4, 4: 2}[mesh.shape["cols"]]
    return side, side, mesh.shape["rows"] // 2


def solution(mesh):
    in_specs = (P("rows", "cols"), P("rows", "cols"), P("cols", None))
    out_specs = (P("rows", "cols"), P("cols", None), P("rows", "cols"))
    return jax.shard_map(
        functools.partial(body, *sizes(mesh)),
        mesh=mesh,
        in_specs=in_specs,
        out_specs=out_specs,
        check_vma=False,
    )
```

```python
import functools

import jax
import jax.numpy as jnp
from jax import lax
from jax.experimental import pallas as pl
from jax.experimental.pallas import tpu as pltpu
from jax.sharding import PartitionSpec as P

D = 8192
RANK = 512
HALF = RANK // 2
BLOCK = 128
MESH = pl.DeviceIdType.MESH
VMEM = pltpu.VMEM
F32 = jnp.float32
FACTOR = D / RANK**0.5


def order(n):
    return sorted(range(1, n), key=lambda d: -min(d, n - d))


class Grid:
    def __init__(self, nx, ny, nz):
        self.n = (nx, ny)
        self.nz = nz
        self.r = lax.axis_index("rows")
        self.c = lax.axis_index("cols")
        self.at = (lax.div(self.c, ny), lax.rem(self.c, ny))
        self.z, self.core = lax.div(self.r, 2), lax.rem(self.r, 2)

    def along(self, axis, d):
        return lax.rem(self.at[axis] + d, self.n[axis])

    def peer(self, axis, d):
        place = [self.at[0], self.at[1]]
        place[axis] = self.along(axis, d)
        return (self.r, place[0] * self.n[1] + place[1])

    def z_along(self, d):
        return lax.rem(self.z + d, self.nz)

    def z_peer(self, d):
        return (self.z_along(d) * 2 + self.core, self.c)

    def sibling(self):
        return (self.r + 1 - 2 * self.core, self.c)

    def cross_peer(self, d, swap):
        core = self.core + swap * (1 - 2 * self.core)
        return (2 * self.z + core, self.along(0, d) * self.n[1] + self.at[1])

    def plane_peers(self):
        return [self.peer(a, d) for a in (0, 1) for d in range(1, self.n[a])]

    def row_peers(self):
        near = [self.z_peer(d) for d in range(1, self.nz)]
        return near + [self.cross_peer(d, 1) for d in range(self.n[0])]


def greet(peers):
    barrier = pltpu.get_barrier_semaphore()
    for device in peers:
        pl.semaphore_signal(barrier, inc=1, device_id=device, device_id_type=MESH)
    return lambda: pl.semaphore_wait(barrier, len(peers))


def send(src, dst, sems, slot, device):
    copy = remote(src, dst, sems, slot, device)
    copy.start()
    return copy


def remote(src, dst, sems, slot, device):
    return pltpu.make_async_remote_copy(
        src_ref=src,
        dst_ref=dst,
        send_sem=sems.at[(0,) + slot],
        recv_sem=sems.at[(1,) + slot],
        device_id=device,
        device_id_type=MESH,
    )


def rowcast(x, k):
    return jnp.broadcast_to(x[k : k + 1, :], (8, BLOCK))


def factor_block(a, x):
    lane = lax.broadcasted_iota(jnp.int32, (8, BLOCK), 1)
    sub = lax.broadcasted_iota(jnp.int32, (8, BLOCK), 0)
    tiles = BLOCK // 8

    def tile(i):
        return slice(8 * i, 8 * i + 8)

    def splats(value, i):
        return [jnp.broadcast_to(value[:, 8 * i + k : 8 * i + k + 1], (8, BLOCK)) for k in range(8)]

    rows = a[tile(0), :]
    columns = splats(rows, 0)
    for t in range(tiles):
        panel = (lane >= 8 * t) & (lane < 8 * t + 8)
        rows = jnp.where(panel, jnp.where(lane == sub + 8 * t, 1.0, 0.0), rows)
        roots, ahead, scaled = [], [], []
        for k in range(8):
            root = lax.rsqrt(rowcast(columns[k], k))
            roots.append(root)
            scaled.append(rowcast(rows, k) * root)
            ahead.append([rowcast(columns[l], k) * root for l in range(k + 1, 8)])
            if k == 7:
                break
            weight = jnp.where(sub > k, columns[k] * root, 0.0)
            for l in range(k + 1, 8):
                columns[l] = columns[l] - weight * ahead[k][l - k - 1]
            rows = rows - weight * scaled[k]
        done = scaled[0]
        for k in range(1, 8):
            done = jnp.where(sub == k, scaled[k], done)
        x[tile(t), :] = jnp.where(lane < 8 * t + 8, done, 0.0)
        for s in range(t + 1, tiles):
            rest = a[tile(s), :]
            below = splats(rest, t)
            following = splats(rest, t + 1) if s == t + 1 else []
            rest = jnp.where(panel, 0.0, rest)
            for k in range(8):
                weight = below[k] * roots[k]
                rest = rest - weight * scaled[k]
                for l in range(k + 1, 8):
                    below[l] = below[l] - weight * ahead[k][l - k - 1]
                if following:
                    following = [v - weight * rowcast(weight, l) for l, v in enumerate(following)]
            if s == t + 1:
                rows, columns = rest, following
            else:
                a[tile(s), :] = rest


def full_dot(a, b, ca, cb):
    return lax.dot_general(
        a, b, (((ca,), (cb,)), ((), ())), precision=lax.Precision.HIGHEST, preferred_element_type=F32
    )


def block(i, size):
    return pl.ds(pl.multiple_of(i * size, size), size)


def arrived(copies):
    for copy in copies:
        copy.wait_recv()


def scatter_power(g, part, rows, recv1, sum1, recv2, sems):
    columns = [pl.ds(h * HALF, HALF) for h in (0, 1)]
    first, second = [[], []], [[], []]

    def strip(h, i):
        return part.at[i, :, :, columns[0]] if h == 0 else part.at[:, i, :, columns[1]]

    for h in (0, 1):
        for d in order(g.n[h]):
            source = strip(h, g.along(h, d))
            first[h].append(send(source, recv1.at[h, d - 1], sems, (0, h, d - 1), g.peer(h, d)))
    for h in (0, 1):
        total = strip(h, g.at[h])[...]
        arrived(first[h])
        for d in range(1, g.n[h]):
            total = total + recv1[h, d - 1]
        sum1[h] = total
        for d in order(g.n[1 - h]):
            source = sum1.at[h, g.along(1 - h, d)]
            second[h].append(
                send(source, recv2.at[h, d - 1], sems, (1, h, d - 1), g.peer(1 - h, d))
            )
    for h in (0, 1):
        total = sum1[h, g.at[1 - h]]
        arrived(second[h])
        for d in range(1, g.n[1 - h]):
            total = total + recv2[h, d - 1]
        rows[:, columns[h]] = total
    return sum(first + second, [])


def factor_gram(a, out, tile, small, between):
    out[...] = jnp.zeros_like(out)

    @pl.loop(0, RANK // BLOCK)
    def _(step):
        tile[...] = a[step, block(step, BLOCK), :]
        factor_block(tile, small)
        for i in range(RANK // BLOCK):

            @pl.when(step == i)
            def _():
                if i < len(between):
                    between[i]()
                low, high = i * BLOCK, (i + 1) * BLOCK
                diagonal = small[...]
                out[low:high, low:high] = diagonal
                if i:
                    out[low:high, :low] = full_dot(diagonal, out[low:high, :low], 1, 0)
                if high < RANK:
                    below = full_dot(a[i, high:, :], diagonal, 1, 1)
                    for j in range(i + 1, RANK // BLOCK):
                        top = (j - i - 1) * BLOCK
                        a[j, j * BLOCK :, :] -= full_dot(
                            below[top:], below[top : top + BLOCK], 1, 1
                        )
                    out[high:, :high] -= full_dot(below, out[low:high, :high], 1, 0)


def step_kernel(
    nx, ny, nz, previous, gradient, q_prev, momentum_next, q_next, update,
    momentum, part, power, recv1, sum1, recv2, near_y, near_x,
    slab, gram_recv, gram_z, whole, a, tile, small, inverse,
    local, cross_core, cross_sum, cross_z, crossed, cross, squares, squares_recv,
    power_sem, near_sem, bulk_sem, gram_sem, core_sem, z_sem, plane_sem, back_sem, norm_sem,
):
    g = Grid(nx, ny, nz)
    x, y = g.at
    core = g.core
    ready = greet(g.plane_peers() + g.row_peers())
    momentum[...] = 0.95 * previous[...] + gradient[...].astype(F32)
    part[...] = full_dot(momentum[...], q_prev[...], 1, 0).reshape(part.shape)
    ready()
    sent = scatter_power(g, part, near_y.at[y], recv1, sum1, recv2, power_sem)

    halves = [pl.ds(h * HALF, HALF) for h in (0, 1)]
    near_x[x] = near_y[y, :, HALF:]
    strips = [[], []]
    for d in order(ny):
        place = near_y.at[y]
        strips[0].append(send(place, place, near_sem, (0, d - 1), g.peer(1, d)))
    for d in order(nx):
        place = near_x.at[x]
        strips[1].append(send(place, place, near_sem, (1, d - 1), g.peer(0, d)))
    arrived(strips[0])

    rows = RANK // (nx * ny)
    group, width = RANK // ny, slab.shape[0]
    own, other = block(core, HALF), block(1 - core, HALF)
    seen = near_y[...].reshape(-1, RANK)
    near_y_part = near_y[:, :, block(lax.div(y * group, width), width)].reshape(-1, width)
    slab[...] = full_dot(near_y_part, seen, 0, 0)
    start = lax.rem(y * group, width)

    def piece(i):
        return pl.ds(pl.multiple_of(start + i * rows, rows), rows)

    spread = []
    for d in order(nx) + [0]:
        for swap in (0, 1):
            if d or swap:
                source = slab.at[piece(g.along(0, d)), other if swap else own]
                slot = 2 * d + swap - 1
                spread.append(
                    send(source, gram_recv.at[slot], gram_sem, (slot,), g.cross_peer(d, swap))
                )

    bulk = [[], []]
    power[x, :, :, halves[0]] = near_y[:, :, :HALF]
    for d in order(nx):
        place = power.at[x, :, :, halves[0]]
        bulk[0].append(
            send(near_y.at[:, :, halves[0]], place, bulk_sem, (0, d - 1), g.peer(0, d))
        )
    arrived(strips[1])
    power[:, y, :, halves[1]] = near_x[...]
    for d in order(ny):
        place = power.at[:, y, :, halves[1]]
        bulk[1].append(send(near_x, place, bulk_sem, (1, d - 1), g.peer(1, d)))

    total = slab[piece(x), own]
    arrived(spread)
    for slot in range(2 * nx - 1):
        total = total + gram_recv[slot]
    gram_z[g.z] = total
    ups = []
    for d in order(nz):
        ups.append(send(gram_z.at[g.z], gram_z.at[g.z], z_sem, (0, d - 1), g.z_peer(d)))
    arrived(ups)
    total = gram_z[0]
    for i in range(1, nz):
        total = total + gram_z[i]
    near, far, back = [[], []], [[], []], [[], []]
    for q in (0, 1):
        place = whole.at[core * 2 + q, y, x]
        whole[core * 2 + q, y, x] = total[:, q * BLOCK : (q + 1) * BLOCK]
        for d in order(g.n[q]):
            near[q].append(send(place, place, plane_sem, (0, q, d - 1), g.peer(q, d)))

    arrived(bulk[0] + bulk[1])
    share = local.shape[0] // nz
    local[...] = full_dot(momentum[...], power[...].reshape(-1, RANK), 0, 0)
    swapped = send(local.at[:, other], cross_core, core_sem, (0,), g.sibling())

    def line(q, i):
        return whole.at[core * 2, i] if q == 0 else whole.at[core * 2 + 1, :, i]

    for q in (0, 1):
        arrived(near[q])
        place = line(q, g.at[1 - q])
        for d in order(g.n[1 - q]):
            far[q].append(send(place, place, plane_sem, (1, q, d - 1), g.peer(1 - q, d)))
        back[q].append(send(place, place, back_sem, (q, 0), g.sibling()))
    swapped.wait_recv()
    cross_sum[...] = local[:, own] + cross_core[...]
    shares = []
    for d in order(nz):
        source = cross_sum.at[block(g.z_along(d), share)]
        shares.append(send(source, cross_z.at[d - 1], z_sem, (1, d - 1), g.z_peer(d)))
    for i in range(nx - 1):
        for q in (0, 1):
            far[q][i].wait_recv()
            d = order(nx)[i]
            place = line(q, g.along(1 - q, g.n[1 - q] - d))
            back[q].append(send(place, place, back_sem, (q, d), g.sibling()))
    arrived(back[0] + back[1])

    mine = block(g.z, share)

    def sum_shares():
        arrived(shares)
        total = cross_sum[mine]
        for d in range(1, nz):
            total = total + cross_z[d - 1]
        crossed[mine, own] = total
        place = crossed.at[mine, own]
        for d in order(nz):
            send(place, place, z_sem, (2, d - 1), g.z_peer(d))

    def gathers():
        place = crossed.at[mine, own]
        return [remote(place, place, z_sem, (2, d - 1), g.z_peer(d)) for d in order(nz)]

    def last():
        place = crossed.at[:, own]
        return remote(place, place, core_sem, (1,), g.sibling())

    def share_sums():
        arrived(gathers())
        last().start()

    a[...] = whole[...].reshape(a.shape)
    factor_gram(a, inverse, tile, small, [sum_shares, share_sums])
    last().wait_recv()

    cross[...] = full_dot(crossed[...], inverse[...], 1, 1)
    squares[0] = jnp.sum(cross[...] * cross[...], axis=0, keepdims=True)
    norms = [[], []]
    for axis in (0, 1):
        for d in order(g.n[axis]):
            place = squares_recv.at[axis, d - 1]
            norms[axis].append(
                send(squares.at[axis], place, norm_sem, (axis, d - 1), g.peer(axis, d))
            )
        if axis == 0:
            turned = full_dot(inverse[...], -0.5 * cross[...], 0, 1)
            momentum_next[...] = momentum[...] + full_dot(
                power[...].reshape(-1, RANK), turned, 1, 0
            )
        arrived(norms[axis])
        total = squares[axis]
        for d in range(1, g.n[axis]):
            total = total + squares_recv[axis, d - 1]
        if axis == 0:
            squares[1] = total
    value = cross[...] / (jnp.sqrt(total) + 1e-08)
    q_next[...] = value
    turned = full_dot(inverse[...], FACTOR * value, 0, 1)
    update[...] = full_dot(power[...].reshape(-1, RANK), turned, 1, 0).astype(update.dtype)
    groups = [sent, spread, ups, shares, gathers(), [swapped, last()]]
    for copy in sum(groups + strips + bulk + near + far + back + norms, []):
        copy.wait_send()


def body(nx, ny, nz, previous, gradient, q_prev):
    height, depth = previous.shape
    rows = RANK // (nx * ny)
    small = height // (nx * ny)
    dma = pltpu.SemaphoreType.DMA
    return pl.pallas_call(
        functools.partial(step_kernel, nx, ny, nz),
        name="power_step",
        out_shape=(
            jax.ShapeDtypeStruct((height, depth), F32),
            jax.ShapeDtypeStruct((depth, RANK), F32),
            jax.ShapeDtypeStruct((height, depth), jnp.bfloat16),
        ),
        in_specs=[pl.BlockSpec(memory_space=VMEM)] * 3,
        out_specs=(pl.BlockSpec(memory_space=VMEM),) * 3,
        scratch_shapes=[
            VMEM((height, depth), F32),
            VMEM((nx, ny, small, RANK), F32),
            VMEM((nx, ny, small, RANK), F32),
            VMEM((2, nx - 1, ny, small, HALF), F32),
            VMEM((2, ny, small, HALF), F32),
            VMEM((2, ny - 1, small, HALF), F32),
            VMEM((ny, small, RANK), F32),
            VMEM((nx, small, HALF), F32),
            VMEM((max(BLOCK, RANK // ny), RANK), F32),
            VMEM((2 * nx - 1, rows, HALF), F32),
            VMEM((nz, rows, HALF), F32),
            VMEM((RANK // BLOCK, ny, nx, rows, BLOCK), F32),
            VMEM((RANK // BLOCK, RANK, BLOCK), F32),
            VMEM((BLOCK, BLOCK), F32),
            VMEM((BLOCK, BLOCK), F32),
            VMEM((RANK, RANK), F32),
            VMEM((depth, RANK), F32),
            VMEM((depth, HALF), F32),
            VMEM((depth, HALF), F32),
            VMEM((nz - 1, depth // nz, HALF), F32),
            VMEM((depth, RANK), F32),
            VMEM((depth, RANK), F32),
            VMEM((2, 1, RANK), F32),
            VMEM((2, nx - 1, 1, RANK), F32),
            dma((2, 2, 2, nx - 1)),
            dma((2, 2, nx - 1)),
            dma((2, 2, nx - 1)),
            dma((2, 2 * nx - 1)),
            dma((2, 2)),
            dma((2, 3, nz - 1)),
            dma((2, 2, 2, nx - 1)),
            dma((2, 2, nx)),
            dma((2, 2, nx - 1)),
        ],
        compiler_params=pltpu.CompilerParams(
            collective_id=0, has_side_effects=True, vmem_limit_bytes=60 << 20
        ),
    )(previous, gradient, q_prev)


def sizes(mesh):
    side = {64: 8, 16: 4, 4: 2}[mesh.shape["cols"]]
    return side, side, mesh.shape["rows"] // 2


def solution(mesh):
    in_specs = (P("rows", "cols"), P("rows", "cols"), P("cols", None))
    out_specs = (P("rows", "cols"), P("cols", None), P("rows", "cols"))
    return jax.shard_map(
        functools.partial(body, *sizes(mesh)),
        mesh=mesh,
        in_specs=in_specs,
        out_specs=out_specs,
        check_vma=False,
    )
```

```python
import functools

import jax
import jax.numpy as jnp
from jax import lax
from jax.experimental import pallas as pl
from jax.experimental.pallas import tpu as pltpu
from jax.sharding import PartitionSpec as P

D = 8192
RANK = 512
HALF = RANK // 2
BLOCK = 128
MESH = pl.DeviceIdType.MESH
VMEM = pltpu.VMEM
F32 = jnp.float32
FACTOR = D / RANK**0.5


def order(n):
    return sorted(range(1, n), key=lambda d: -min(d, n - d))


class Grid:
    def __init__(self, nx, ny, nz):
        self.n = (nx, ny)
        self.nz = nz
        self.r = lax.axis_index("rows")
        self.c = lax.axis_index("cols")
        self.at = (lax.div(self.c, ny), lax.rem(self.c, ny))
        self.z, self.core = lax.div(self.r, 2), lax.rem(self.r, 2)

    def along(self, axis, d):
        return lax.rem(self.at[axis] + d, self.n[axis])

    def peer(self, axis, d):
        place = [self.at[0], self.at[1]]
        place[axis] = self.along(axis, d)
        return (self.r, place[0] * self.n[1] + place[1])

    def z_along(self, d):
        return lax.rem(self.z + d, self.nz)

    def z_peer(self, d):
        return (self.z_along(d) * 2 + self.core, self.c)

    def sibling(self):
        return (self.r + 1 - 2 * self.core, self.c)

    def cross_peer(self, d, swap):
        core = self.core + swap * (1 - 2 * self.core)
        return (2 * self.z + core, self.along(0, d) * self.n[1] + self.at[1])

    def plane_peers(self):
        return [self.peer(a, d) for a in (0, 1) for d in range(1, self.n[a])]

    def row_peers(self):
        near = [self.z_peer(d) for d in range(1, self.nz)]
        return near + [self.cross_peer(d, 1) for d in range(self.n[0])]


def greet(peers):
    barrier = pltpu.get_barrier_semaphore()
    for device in peers:
        pl.semaphore_signal(barrier, inc=1, device_id=device, device_id_type=MESH)
    return lambda: pl.semaphore_wait(barrier, len(peers))


def send(src, dst, sems, slot, device):
    copy = remote(src, dst, sems, slot, device)
    copy.start()
    return copy


def remote(src, dst, sems, slot, device):
    return pltpu.make_async_remote_copy(
        src_ref=src,
        dst_ref=dst,
        send_sem=sems.at[(0,) + slot],
        recv_sem=sems.at[(1,) + slot],
        device_id=device,
        device_id_type=MESH,
    )


def rowcast(x, k):
    return jnp.broadcast_to(x[k : k + 1, :], (8, BLOCK))


def factor_block(a, x):
    lane = lax.broadcasted_iota(jnp.int32, (8, BLOCK), 1)
    sub = lax.broadcasted_iota(jnp.int32, (8, BLOCK), 0)
    tiles = BLOCK // 8

    def tile(i):
        return slice(8 * i, 8 * i + 8)

    def splats(value, i):
        return [jnp.broadcast_to(value[:, 8 * i + k : 8 * i + k + 1], (8, BLOCK)) for k in range(8)]

    rows = a[tile(0), :]
    columns = splats(rows, 0)
    for t in range(tiles):
        panel = (lane >= 8 * t) & (lane < 8 * t + 8)
        rows = jnp.where(panel, jnp.where(lane == sub + 8 * t, 1.0, 0.0), rows)
        roots, ahead, scaled = [], [], []
        for k in range(8):
            root = lax.rsqrt(rowcast(columns[k], k))
            roots.append(root)
            scaled.append(rowcast(rows, k) * root)
            ahead.append([rowcast(columns[l], k) * root for l in range(k + 1, 8)])
            if k == 7:
                break
            weight = jnp.where(sub > k, columns[k] * root, 0.0)
            for l in range(k + 1, 8):
                columns[l] = columns[l] - weight * ahead[k][l - k - 1]
            rows = rows - weight * scaled[k]
        done = scaled[0]
        for k in range(1, 8):
            done = jnp.where(sub == k, scaled[k], done)
        x[tile(t), :] = jnp.where(lane < 8 * t + 8, done, 0.0)
        for s in range(t + 1, tiles):
            rest = a[tile(s), :]
            below = splats(rest, t)
            following = splats(rest, t + 1) if s == t + 1 else []
            rest = jnp.where(panel, 0.0, rest)
            for k in range(8):
                weight = below[k] * roots[k]
                rest = rest - weight * scaled[k]
                for l in range(k + 1, 8):
                    below[l] = below[l] - weight * ahead[k][l - k - 1]
                if following:
                    following = [v - weight * rowcast(weight, l) for l, v in enumerate(following)]
            if s == t + 1:
                rows, columns = rest, following
            else:
                a[tile(s), :] = rest


def full_dot(a, b, ca, cb):
    return lax.dot_general(
        a, b, (((ca,), (cb,)), ((), ())), precision=lax.Precision.HIGHEST, preferred_element_type=F32
    )


def block(i, size):
    return pl.ds(pl.multiple_of(i * size, size), size)


def arrived(copies):
    for copy in copies:
        copy.wait_recv()


def scatter_power(g, part, rows, recv1, sum1, recv2, sems):
    columns = [pl.ds(h * HALF, HALF) for h in (0, 1)]
    first, second = [[], []], [[], []]

    def strip(h, i):
        return part.at[i, :, :, columns[0]] if h == 0 else part.at[:, i, :, columns[1]]

    for h in (0, 1):
        for d in order(g.n[h]):
            source = strip(h, g.along(h, d))
            first[h].append(send(source, recv1.at[h, d - 1], sems, (0, h, d - 1), g.peer(h, d)))
    for h in (0, 1):
        total = strip(h, g.at[h])[...]
        arrived(first[h])
        for d in range(1, g.n[h]):
            total = total + recv1[h, d - 1]
        sum1[h] = total
        for d in order(g.n[1 - h]):
            source = sum1.at[h, g.along(1 - h, d)]
            second[h].append(
                send(source, recv2.at[h, d - 1], sems, (1, h, d - 1), g.peer(1 - h, d))
            )
    for h in (0, 1):
        total = sum1[h, g.at[1 - h]]
        arrived(second[h])
        for d in range(1, g.n[1 - h]):
            total = total + recv2[h, d - 1]
        rows[:, columns[h]] = total
    return sum(first + second, [])


def factor_gram(a, out, tile, small, between):
    out[...] = jnp.zeros_like(out)

    @pl.loop(0, RANK // BLOCK)
    def _(step):
        tile[...] = a[step, block(step, BLOCK), :]
        factor_block(tile, small)
        for i in range(RANK // BLOCK):

            @pl.when(step == i)
            def _():
                if i < len(between):
                    between[i]()
                low, high = i * BLOCK, (i + 1) * BLOCK
                diagonal = small[...]
                out[low:high, low:high] = diagonal
                if i:
                    out[low:high, :low] = full_dot(diagonal, out[low:high, :low], 1, 0)
                if high < RANK:
                    below = full_dot(a[i, high:, :], diagonal, 1, 1)
                    for j in range(i + 1, RANK // BLOCK):
                        top = (j - i - 1) * BLOCK
                        a[j, j * BLOCK :, :] -= full_dot(
                            below[top:], below[top : top + BLOCK], 1, 1
                        )
                    out[high:, :high] -= full_dot(below, out[low:high, :high], 1, 0)


def step_kernel(
    nx, ny, nz, momentum, q_prev, basis, cross, col_sq,
    part, power, recv1, sum1, recv2, near_y, near_x,
    slab, gram_recv, gram_z, whole, a, tile, small, inverse,
    local, cross_core, cross_sum, cross_z, crossed, squares, squares_recv,
    power_sem, near_sem, bulk_sem, gram_sem, core_sem, z_sem, plane_sem, back_sem, norm_sem,
):
    g = Grid(nx, ny, nz)
    x, y = g.at
    core = g.core
    ready = greet(g.plane_peers() + g.row_peers())
    part[...] = full_dot(momentum[...], q_prev[...], 1, 0).reshape(part.shape)
    ready()
    sent = scatter_power(g, part, near_y.at[y], recv1, sum1, recv2, power_sem)

    halves = [pl.ds(h * HALF, HALF) for h in (0, 1)]
    near_x[x] = near_y[y, :, HALF:]
    strips = [[], []]
    for d in order(ny):
        place = near_y.at[y]
        strips[0].append(send(place, place, near_sem, (0, d - 1), g.peer(1, d)))
    for d in order(nx):
        place = near_x.at[x]
        strips[1].append(send(place, place, near_sem, (1, d - 1), g.peer(0, d)))
    arrived(strips[0])

    rows = RANK // (nx * ny)
    group, width = RANK // ny, slab.shape[0]
    own, other = block(core, HALF), block(1 - core, HALF)
    seen = near_y[...].reshape(-1, RANK)
    near_y_part = near_y[:, :, block(lax.div(y * group, width), width)].reshape(-1, width)
    slab[...] = full_dot(near_y_part, seen, 0, 0)
    start = lax.rem(y * group, width)

    def piece(i):
        return pl.ds(pl.multiple_of(start + i * rows, rows), rows)

    spread = []
    for d in order(nx) + [0]:
        for swap in (0, 1):
            if d or swap:
                source = slab.at[piece(g.along(0, d)), other if swap else own]
                slot = 2 * d + swap - 1
                spread.append(
                    send(source, gram_recv.at[slot], gram_sem, (slot,), g.cross_peer(d, swap))
                )

    bulk = [[], []]
    power[x, :, :, halves[0]] = near_y[:, :, :HALF]
    for d in order(nx):
        place = power.at[x, :, :, halves[0]]
        bulk[0].append(
            send(near_y.at[:, :, halves[0]], place, bulk_sem, (0, d - 1), g.peer(0, d))
        )
    arrived(strips[1])
    power[:, y, :, halves[1]] = near_x[...]
    for d in order(ny):
        place = power.at[:, y, :, halves[1]]
        bulk[1].append(send(near_x, place, bulk_sem, (1, d - 1), g.peer(1, d)))

    total = slab[piece(x), own]
    arrived(spread)
    for slot in range(2 * nx - 1):
        total = total + gram_recv[slot]
    gram_z[g.z] = total
    ups = []
    for d in order(nz):
        ups.append(send(gram_z.at[g.z], gram_z.at[g.z], z_sem, (0, d - 1), g.z_peer(d)))
    arrived(ups)
    total = gram_z[0]
    for i in range(1, nz):
        total = total + gram_z[i]
    near, far, back = [[], []], [[], []], [[], []]
    for q in (0, 1):
        place = whole.at[core * 2 + q, y, x]
        whole[core * 2 + q, y, x] = total[:, q * BLOCK : (q + 1) * BLOCK]
        for d in order(g.n[q]):
            near[q].append(send(place, place, plane_sem, (0, q, d - 1), g.peer(q, d)))

    arrived(bulk[0] + bulk[1])
    share = local.shape[0] // nz
    local[...] = full_dot(momentum[...], power[...].reshape(-1, RANK), 0, 0)
    swapped = send(local.at[:, other], cross_core, core_sem, (0,), g.sibling())

    def line(q, i):
        return whole.at[core * 2, i] if q == 0 else whole.at[core * 2 + 1, :, i]

    for q in (0, 1):
        arrived(near[q])
        place = line(q, g.at[1 - q])
        for d in order(g.n[1 - q]):
            far[q].append(send(place, place, plane_sem, (1, q, d - 1), g.peer(1 - q, d)))
        back[q].append(send(place, place, back_sem, (q, 0), g.sibling()))
    swapped.wait_recv()
    cross_sum[...] = local[:, own] + cross_core[...]
    shares = []
    for d in order(nz):
        source = cross_sum.at[block(g.z_along(d), share)]
        shares.append(send(source, cross_z.at[d - 1], z_sem, (1, d - 1), g.z_peer(d)))
    for i in range(nx - 1):
        for q in (0, 1):
            far[q][i].wait_recv()
            d = order(nx)[i]
            place = line(q, g.along(1 - q, g.n[1 - q] - d))
            back[q].append(send(place, place, back_sem, (q, d), g.sibling()))
    arrived(back[0] + back[1])

    mine = block(g.z, share)

    def sum_shares():
        arrived(shares)
        total = cross_sum[mine]
        for d in range(1, nz):
            total = total + cross_z[d - 1]
        crossed[mine, own] = total
        place = crossed.at[mine, own]
        for d in order(nz):
            send(place, place, z_sem, (2, d - 1), g.z_peer(d))

    def gathers():
        place = crossed.at[mine, own]
        return [remote(place, place, z_sem, (2, d - 1), g.z_peer(d)) for d in order(nz)]

    def last():
        place = crossed.at[:, own]
        return remote(place, place, core_sem, (1,), g.sibling())

    def share_sums():
        arrived(gathers())
        last().start()

    a[...] = whole[...].reshape(a.shape)
    factor_gram(a, inverse, tile, small, [sum_shares, share_sums])
    last().wait_recv()

    value = full_dot(crossed[...], inverse[...], 1, 1)
    cross[...] = value
    squares[0] = jnp.sum(value * value, axis=0, keepdims=True)
    norms = [[], []]
    for axis in (0, 1):
        for d in order(g.n[axis]):
            place = squares_recv.at[axis, d - 1]
            norms[axis].append(
                send(squares.at[axis], place, norm_sem, (axis, d - 1), g.peer(axis, d))
            )
        if axis == 0:
            basis[...] = full_dot(power[...].reshape(-1, RANK), inverse[...], 1, 1)
        arrived(norms[axis])
        total = squares[axis]
        for d in range(1, g.n[axis]):
            total = total + squares_recv[axis, d - 1]
        if axis == 0:
            squares[1] = total
    col_sq[...] = total
    groups = [sent, spread, ups, shares, gathers(), [swapped, last()]]
    for copy in sum(groups + strips + bulk + near + far + back + norms, []):
        copy.wait_send()


def finish_kernel(momentum, basis, cross, col_sq, momentum_next, q_next, update):
    momentum_next[...] = momentum[...] - 0.5 * full_dot(basis[...], cross[...], 1, 1)
    value = cross[...] / (jnp.sqrt(col_sq[...]) + 1e-08)
    q_next[...] = value
    update[...] = (FACTOR * full_dot(basis[...], value, 1, 1)).astype(update.dtype)


def body(nx, ny, nz, previous, gradient, q_prev):
    height, depth = previous.shape
    momentum = 0.95 * previous + gradient.astype(F32)
    rows = RANK // (nx * ny)
    small = height // (nx * ny)
    dma = pltpu.SemaphoreType.DMA
    basis, cross, col_sq = pl.pallas_call(
        functools.partial(step_kernel, nx, ny, nz),
        name="power_step",
        out_shape=(
            jax.ShapeDtypeStruct((height, RANK), F32),
            jax.ShapeDtypeStruct((depth, RANK), F32),
            jax.ShapeDtypeStruct((1, RANK), F32),
        ),
        in_specs=[pl.BlockSpec(memory_space=VMEM)] * 2,
        out_specs=(pl.BlockSpec(memory_space=VMEM),) * 3,
        scratch_shapes=[
            VMEM((nx, ny, small, RANK), F32),
            VMEM((nx, ny, small, RANK), F32),
            VMEM((2, nx - 1, ny, small, HALF), F32),
            VMEM((2, ny, small, HALF), F32),
            VMEM((2, ny - 1, small, HALF), F32),
            VMEM((ny, small, RANK), F32),
            VMEM((nx, small, HALF), F32),
            VMEM((max(BLOCK, RANK // ny), RANK), F32),
            VMEM((2 * nx - 1, rows, HALF), F32),
            VMEM((nz, rows, HALF), F32),
            VMEM((RANK // BLOCK, ny, nx, rows, BLOCK), F32),
            VMEM((RANK // BLOCK, RANK, BLOCK), F32),
            VMEM((BLOCK, BLOCK), F32),
            VMEM((BLOCK, BLOCK), F32),
            VMEM((RANK, RANK), F32),
            VMEM((depth, RANK), F32),
            VMEM((depth, HALF), F32),
            VMEM((depth, HALF), F32),
            VMEM((nz - 1, depth // nz, HALF), F32),
            VMEM((depth, RANK), F32),
            VMEM((2, 1, RANK), F32),
            VMEM((2, nx - 1, 1, RANK), F32),
            dma((2, 2, 2, nx - 1)),
            dma((2, 2, nx - 1)),
            dma((2, 2, nx - 1)),
            dma((2, 2 * nx - 1)),
            dma((2, 2)),
            dma((2, 3, nz - 1)),
            dma((2, 2, 2, nx - 1)),
            dma((2, 2, nx)),
            dma((2, 2, nx - 1)),
        ],
        compiler_params=pltpu.CompilerParams(
            collective_id=0, has_side_effects=True, vmem_limit_bytes=40 << 20
        ),
    )(momentum, q_prev)
    return pl.pallas_call(
        finish_kernel,
        name="finish",
        out_shape=(
            jax.ShapeDtypeStruct((height, depth), F32),
            jax.ShapeDtypeStruct((depth, RANK), F32),
            jax.ShapeDtypeStruct((height, depth), jnp.bfloat16),
        ),
        in_specs=[pl.BlockSpec(memory_space=VMEM)] * 4,
        out_specs=(pl.BlockSpec(memory_space=VMEM),) * 3,
        compiler_params=pltpu.CompilerParams(vmem_limit_bytes=24 << 20),
    )(momentum, basis, cross, col_sq)


def sizes(mesh):
    side = {64: 8, 16: 4, 4: 2}[mesh.shape["cols"]]
    return side, side, mesh.shape["rows"] // 2


def solution(mesh):
    in_specs = (P("rows", "cols"), P("rows", "cols"), P("cols", None))
    out_specs = (P("rows", "cols"), P("cols", None), P("rows", "cols"))
    return jax.shard_map(
        functools.partial(body, *sizes(mesh)),
        mesh=mesh,
        in_specs=in_specs,
        out_specs=out_specs,
        check_vma=False,
    )
```

```python
import functools

import jax
import jax.numpy as jnp
from jax import lax
from jax.experimental import pallas as pl
from jax.experimental.pallas import tpu as pltpu
from jax.sharding import PartitionSpec as P

D = 8192
RANK = 512
HALF = RANK // 2
BLOCK = 128
MESH = pl.DeviceIdType.MESH
VMEM = pltpu.VMEM
F32 = jnp.float32
FACTOR = D / RANK**0.5


def order(n):
    return sorted(range(1, n), key=lambda d: -min(d, n - d))


class Grid:
    def __init__(self, nx, ny, nz):
        self.n = (nx, ny)
        self.nz = nz
        self.r = lax.axis_index("rows")
        self.c = lax.axis_index("cols")
        self.at = (lax.div(self.c, ny), lax.rem(self.c, ny))
        self.z, self.core = lax.div(self.r, 2), lax.rem(self.r, 2)

    def along(self, axis, d):
        return lax.rem(self.at[axis] + d, self.n[axis])

    def peer(self, axis, d):
        place = [self.at[0], self.at[1]]
        place[axis] = self.along(axis, d)
        return (self.r, place[0] * self.n[1] + place[1])

    def z_along(self, d):
        return lax.rem(self.z + d, self.nz)

    def z_peer(self, d):
        return (self.z_along(d) * 2 + self.core, self.c)

    def sibling(self):
        return (self.r + 1 - 2 * self.core, self.c)

    def cross_peer(self, d, swap):
        core = self.core + swap * (1 - 2 * self.core)
        return (2 * self.z + core, self.along(0, d) * self.n[1] + self.at[1])

    def plane_peers(self):
        return [self.peer(a, d) for a in (0, 1) for d in range(1, self.n[a])]

    def row_peers(self):
        near = [self.z_peer(d) for d in range(1, self.nz)]
        return near + [self.cross_peer(d, 1) for d in range(self.n[0])]


def greet(peers):
    barrier = pltpu.get_barrier_semaphore()
    for device in peers:
        pl.semaphore_signal(barrier, inc=1, device_id=device, device_id_type=MESH)
    return lambda: pl.semaphore_wait(barrier, len(peers))


def send(src, dst, sems, slot, device):
    copy = remote(src, dst, sems, slot, device)
    copy.start()
    return copy


def remote(src, dst, sems, slot, device):
    return pltpu.make_async_remote_copy(
        src_ref=src,
        dst_ref=dst,
        send_sem=sems.at[(0,) + slot],
        recv_sem=sems.at[(1,) + slot],
        device_id=device,
        device_id_type=MESH,
    )


def rowcast(x, k):
    return jnp.broadcast_to(x[k : k + 1, :], (8, BLOCK))


def factor_block(a, x):
    lane = lax.broadcasted_iota(jnp.int32, (8, BLOCK), 1)
    sub = lax.broadcasted_iota(jnp.int32, (8, BLOCK), 0)
    tiles = BLOCK // 8

    def tile(i):
        return slice(8 * i, 8 * i + 8)

    def splats(value, i):
        return [jnp.broadcast_to(value[:, 8 * i + k : 8 * i + k + 1], (8, BLOCK)) for k in range(8)]

    rows = a[tile(0), :]
    columns = splats(rows, 0)
    for t in range(tiles):
        panel = (lane >= 8 * t) & (lane < 8 * t + 8)
        rows = jnp.where(panel, jnp.where(lane == sub + 8 * t, 1.0, 0.0), rows)
        roots, ahead, scaled = [], [], []
        for k in range(8):
            root = lax.rsqrt(rowcast(columns[k], k))
            roots.append(root)
            scaled.append(rowcast(rows, k) * root)
            ahead.append([rowcast(columns[l], k) * root for l in range(k + 1, 8)])
            if k == 7:
                break
            weight = jnp.where(sub > k, columns[k] * root, 0.0)
            for l in range(k + 1, 8):
                columns[l] = columns[l] - weight * ahead[k][l - k - 1]
            rows = rows - weight * scaled[k]
        done = scaled[0]
        for k in range(1, 8):
            done = jnp.where(sub == k, scaled[k], done)
        x[tile(t), :] = jnp.where(lane < 8 * t + 8, done, 0.0)
        for s in range(t + 1, tiles):
            rest = a[tile(s), :]
            below = splats(rest, t)
            following = splats(rest, t + 1) if s == t + 1 else []
            rest = jnp.where(panel, 0.0, rest)
            for k in range(8):
                weight = below[k] * roots[k]
                rest = rest - weight * scaled[k]
                for l in range(k + 1, 8):
                    below[l] = below[l] - weight * ahead[k][l - k - 1]
                if following:
                    following = [v - weight * rowcast(weight, l) for l, v in enumerate(following)]
            if s == t + 1:
                rows, columns = rest, following
            else:
                a[tile(s), :] = rest


def full_dot(a, b, ca, cb):
    return lax.dot_general(
        a, b, (((ca,), (cb,)), ((), ())), precision=lax.Precision.HIGHEST, preferred_element_type=F32
    )


def block(i, size):
    return pl.ds(pl.multiple_of(i * size, size), size)


def arrived(copies):
    for copy in copies:
        copy.wait_recv()


def scatter_power(g, part, rows, recv1, relayed, sum1, recv2, sems):
    columns = [pl.ds(h * HALF, HALF) for h in (0, 1)]
    first, second = [[], []], [[], []]

    def strip(h, i):
        return part.at[i, :, :, columns[0]] if h == 0 else part.at[:, i, :, columns[1]]

    relays = [[], []]
    for h in (0, 1):
        n = g.n[h]
        half = n // 2 if n >= 4 else n
        if half < n:
            source = strip(h, g.along(h, half))
            relays[h].append(send(source, relayed.at[0, h], sems, (2, h, 0), g.peer(h, n - 1)))
        for d in order(n):
            if d not in (half, half + 1):
                source = strip(h, g.along(h, d))
                first[h].append(send(source, recv1.at[h, d - 1], sems, (0, h, d - 1), g.peer(h, d)))
    for h in (0, 1):
        arrived(relays[h])
        if relays[h]:
            d = g.n[h] // 2 + 1
            relayed[1, h] = strip(h, g.along(h, d))[...] + relayed[0, h]
            source = relayed.at[1, h]
            first[h].append(send(source, recv1.at[h, d - 1], sems, (0, h, d - 1), g.peer(h, d)))
    for h in (0, 1):
        total = strip(h, g.at[h])[...]
        arrived(first[h])
        for d in range(1, g.n[h]):
            if not relays[h] or d != g.n[h] // 2:
                total = total + recv1[h, d - 1]
        sum1[h] = total
        for d in order(g.n[1 - h]):
            source = sum1.at[h, g.along(1 - h, d)]
            second[h].append(
                send(source, recv2.at[h, d - 1], sems, (1, h, d - 1), g.peer(1 - h, d))
            )
    for h in (0, 1):
        total = sum1[h, g.at[1 - h]]
        arrived(second[h])
        for d in range(1, g.n[1 - h]):
            total = total + recv2[h, d - 1]
        rows[:, columns[h]] = total
    return sum(first + second + relays, [])


def factor_gram(a, out, tile, small, between):
    out[...] = jnp.zeros_like(out)

    @pl.loop(0, RANK // BLOCK)
    def _(step):
        tile[...] = a[step, block(step, BLOCK), :]
        factor_block(tile, small)
        for i in range(RANK // BLOCK):

            @pl.when(step == i)
            def _():
                if i < len(between):
                    between[i]()
                low, high = i * BLOCK, (i + 1) * BLOCK
                diagonal = small[...]
                out[low:high, low:high] = diagonal
                if i:
                    out[low:high, :low] = full_dot(diagonal, out[low:high, :low], 1, 0)
                if high < RANK:
                    below = full_dot(a[i, high:, :], diagonal, 1, 1)
                    for j in range(i + 1, RANK // BLOCK):
                        top = (j - i - 1) * BLOCK
                        a[j, j * BLOCK :, :] -= full_dot(
                            below[top:], below[top : top + BLOCK], 1, 1
                        )
                    out[high:, :high] -= full_dot(below, out[low:high, :high], 1, 0)


def step_kernel(
    nx, ny, nz, momentum, q_prev, basis, cross, col_sq,
    part, power, recv1, relayed, sum1, recv2, near_y, near_x,
    slab, gram_recv, gram_z, whole, a, tile, small, inverse,
    local, cross_core, cross_sum, cross_z, crossed, squares, squares_recv,
    power_sem, near_sem, bulk_sem, gram_sem, core_sem, z_sem, plane_sem, back_sem, norm_sem,
):
    g = Grid(nx, ny, nz)
    x, y = g.at
    core = g.core
    ready = greet(g.plane_peers() + g.row_peers())
    part[...] = full_dot(momentum[...], q_prev[...], 1, 0).reshape(part.shape)
    ready()
    sent = scatter_power(g, part, near_y.at[y], recv1, relayed, sum1, recv2, power_sem)

    halves = [pl.ds(h * HALF, HALF) for h in (0, 1)]
    near_x[x] = near_y[y, :, HALF:]
    strips = [[], []]
    for d in order(ny):
        place = near_y.at[y]
        strips[0].append(send(place, place, near_sem, (0, d - 1), g.peer(1, d)))
    for d in order(nx):
        place = near_x.at[x]
        strips[1].append(send(place, place, near_sem, (1, d - 1), g.peer(0, d)))
    arrived(strips[0])

    rows = RANK // (nx * ny)
    group, width = RANK // ny, slab.shape[0]
    own, other = block(core, HALF), block(1 - core, HALF)
    seen = near_y[...].reshape(-1, RANK)
    near_y_part = near_y[:, :, block(lax.div(y * group, width), width)].reshape(-1, width)
    slab[...] = full_dot(near_y_part, seen, 0, 0)
    start = lax.rem(y * group, width)

    def piece(i):
        return pl.ds(pl.multiple_of(start + i * rows, rows), rows)

    spread = []
    for d in order(nx) + [0]:
        for swap in (0, 1):
            if d or swap:
                source = slab.at[piece(g.along(0, d)), other if swap else own]
                slot = 2 * d + swap - 1
                spread.append(
                    send(source, gram_recv.at[slot], gram_sem, (slot,), g.cross_peer(d, swap))
                )

    bulk = [[], []]
    power[x, :, :, halves[0]] = near_y[:, :, :HALF]
    for d in order(nx):
        place = power.at[x, :, :, halves[0]]
        bulk[0].append(
            send(near_y.at[:, :, halves[0]], place, bulk_sem, (0, d - 1), g.peer(0, d))
        )
    arrived(strips[1])
    power[:, y, :, halves[1]] = near_x[...]
    for d in order(ny):
        place = power.at[:, y, :, halves[1]]
        bulk[1].append(send(near_x, place, bulk_sem, (1, d - 1), g.peer(1, d)))

    total = slab[piece(x), own]
    arrived(spread)
    for slot in range(2 * nx - 1):
        total = total + gram_recv[slot]
    gram_z[g.z] = total
    ups = []
    for d in order(nz):
        ups.append(send(gram_z.at[g.z], gram_z.at[g.z], z_sem, (0, d - 1), g.z_peer(d)))
    arrived(ups)
    total = gram_z[0]
    for i in range(1, nz):
        total = total + gram_z[i]
    near, far, back = [[], []], [[], []], [[], []]
    for q in (0, 1):
        place = whole.at[core * 2 + q, y, x]
        whole[core * 2 + q, y, x] = total[:, q * BLOCK : (q + 1) * BLOCK]
        for d in order(g.n[q]):
            near[q].append(send(place, place, plane_sem, (0, q, d - 1), g.peer(q, d)))

    arrived(bulk[0] + bulk[1])
    share = local.shape[0] // nz
    local[...] = full_dot(momentum[...], power[...].reshape(-1, RANK), 0, 0)
    swapped = send(local.at[:, other], cross_core, core_sem, (0,), g.sibling())

    def line(q, i):
        return whole.at[core * 2, i] if q == 0 else whole.at[core * 2 + 1, :, i]

    for q in (0, 1):
        arrived(near[q])
        place = line(q, g.at[1 - q])
        for d in order(g.n[1 - q]):
            far[q].append(send(place, place, plane_sem, (1, q, d - 1), g.peer(1 - q, d)))
        back[q].append(send(place, place, back_sem, (q, 0), g.sibling()))
    swapped.wait_recv()
    cross_sum[...] = local[:, own] + cross_core[...]
    shares = []
    for d in order(nz):
        source = cross_sum.at[block(g.z_along(d), share)]
        shares.append(send(source, cross_z.at[d - 1], z_sem, (1, d - 1), g.z_peer(d)))
    for i in range(nx - 1):
        for q in (0, 1):
            far[q][i].wait_recv()
            d = order(nx)[i]
            place = line(q, g.along(1 - q, g.n[1 - q] - d))
            back[q].append(send(place, place, back_sem, (q, d), g.sibling()))
    arrived(back[0] + back[1])

    mine = block(g.z, share)

    def sum_shares():
        arrived(shares)
        total = cross_sum[mine]
        for d in range(1, nz):
            total = total + cross_z[d - 1]
        crossed[mine, own] = total
        place = crossed.at[mine, own]
        for d in order(nz):
            send(place, place, z_sem, (2, d - 1), g.z_peer(d))

    def gathers():
        place = crossed.at[mine, own]
        return [remote(place, place, z_sem, (2, d - 1), g.z_peer(d)) for d in order(nz)]

    def last():
        place = crossed.at[:, own]
        return remote(place, place, core_sem, (1,), g.sibling())

    def share_sums():
        arrived(gathers())
        last().start()

    a[...] = whole[...].reshape(a.shape)
    factor_gram(a, inverse, tile, small, [sum_shares, share_sums])
    last().wait_recv()

    value = full_dot(crossed[...], inverse[...], 1, 1)
    cross[...] = value
    squares[0] = jnp.sum(value * value, axis=0, keepdims=True)
    norms = [[], []]
    for axis in (0, 1):
        for d in order(g.n[axis]):
            place = squares_recv.at[axis, d - 1]
            norms[axis].append(
                send(squares.at[axis], place, norm_sem, (axis, d - 1), g.peer(axis, d))
            )
        if axis == 0:
            basis[...] = full_dot(power[...].reshape(-1, RANK), inverse[...], 1, 1)
        arrived(norms[axis])
        total = squares[axis]
        for d in range(1, g.n[axis]):
            total = total + squares_recv[axis, d - 1]
        if axis == 0:
            squares[1] = total
    col_sq[...] = total
    groups = [sent, spread, ups, shares, gathers(), [swapped, last()]]
    for copy in sum(groups + strips + bulk + near + far + back + norms, []):
        copy.wait_send()


def finish_kernel(momentum, basis, cross, col_sq, momentum_next, q_next, update):
    momentum_next[...] = momentum[...] - 0.5 * full_dot(basis[...], cross[...], 1, 1)
    value = cross[...] / (jnp.sqrt(col_sq[...]) + 1e-08)
    q_next[...] = value
    update[...] = (FACTOR * full_dot(basis[...], value, 1, 1)).astype(update.dtype)


def body(nx, ny, nz, previous, gradient, q_prev):
    height, depth = previous.shape
    momentum = 0.95 * previous + gradient.astype(F32)
    rows = RANK // (nx * ny)
    small = height // (nx * ny)
    dma = pltpu.SemaphoreType.DMA
    basis, cross, col_sq = pl.pallas_call(
        functools.partial(step_kernel, nx, ny, nz),
        name="power_step",
        out_shape=(
            jax.ShapeDtypeStruct((height, RANK), F32),
            jax.ShapeDtypeStruct((depth, RANK), F32),
            jax.ShapeDtypeStruct((1, RANK), F32),
        ),
        in_specs=[pl.BlockSpec(memory_space=VMEM)] * 2,
        out_specs=(pl.BlockSpec(memory_space=VMEM),) * 3,
        scratch_shapes=[
            VMEM((nx, ny, small, RANK), F32),
            VMEM((nx, ny, small, RANK), F32),
            VMEM((2, nx - 1, ny, small, HALF), F32),
            VMEM((2, 2, ny, small, HALF), F32),
            VMEM((2, ny, small, HALF), F32),
            VMEM((2, ny - 1, small, HALF), F32),
            VMEM((ny, small, RANK), F32),
            VMEM((nx, small, HALF), F32),
            VMEM((max(BLOCK, RANK // ny), RANK), F32),
            VMEM((2 * nx - 1, rows, HALF), F32),
            VMEM((nz, rows, HALF), F32),
            VMEM((RANK // BLOCK, ny, nx, rows, BLOCK), F32),
            VMEM((RANK // BLOCK, RANK, BLOCK), F32),
            VMEM((BLOCK, BLOCK), F32),
            VMEM((BLOCK, BLOCK), F32),
            VMEM((RANK, RANK), F32),
            VMEM((depth, RANK), F32),
            VMEM((depth, HALF), F32),
            VMEM((depth, HALF), F32),
            VMEM((nz - 1, depth // nz, HALF), F32),
            VMEM((depth, RANK), F32),
            VMEM((2, 1, RANK), F32),
            VMEM((2, nx - 1, 1, RANK), F32),
            dma((2, 3, 2, nx - 1)),
            dma((2, 2, nx - 1)),
            dma((2, 2, nx - 1)),
            dma((2, 2 * nx - 1)),
            dma((2, 2)),
            dma((2, 3, nz - 1)),
            dma((2, 2, 2, nx - 1)),
            dma((2, 2, nx)),
            dma((2, 2, nx - 1)),
        ],
        compiler_params=pltpu.CompilerParams(
            collective_id=0, has_side_effects=True, vmem_limit_bytes=40 << 20
        ),
    )(momentum, q_prev)
    return pl.pallas_call(
        finish_kernel,
        name="finish",
        out_shape=(
            jax.ShapeDtypeStruct((height, depth), F32),
            jax.ShapeDtypeStruct((depth, RANK), F32),
            jax.ShapeDtypeStruct((height, depth), jnp.bfloat16),
        ),
        in_specs=[pl.BlockSpec(memory_space=VMEM)] * 4,
        out_specs=(pl.BlockSpec(memory_space=VMEM),) * 3,
        compiler_params=pltpu.CompilerParams(vmem_limit_bytes=24 << 20),
    )(momentum, basis, cross, col_sq)


def sizes(mesh):
    side = {64: 8, 16: 4, 4: 2}[mesh.shape["cols"]]
    return side, side, mesh.shape["rows"] // 2


def solution(mesh):
    in_specs = (P("rows", "cols"), P("rows", "cols"), P("cols", None))
    out_specs = (P("rows", "cols"), P("cols", None), P("rows", "cols"))
    return jax.shard_map(
        functools.partial(body, *sizes(mesh)),
        mesh=mesh,
        in_specs=in_specs,
        out_specs=out_specs,
        check_vma=False,
    )
```
